512 devices in a mesh: doc: 8 (over y, core), ctx: 64 (over x, z).
Axes of the slice: x: 4, y: 4, z: 16, core: 2. Of those that a mesh axis runs over, the one named last changes fastest.
Arguments:
- ctx_query: bfloat16 [131072, 2048], P(('doc', 'ctx')), parts along dimension 0, may hold values from -6 to 6
- ctx_key: bfloat16 [131072, 512], P(('doc', 'ctx')), parts along dimension 0, may hold values from -256 to 256
- ctx_value: bfloat16 [131072, 512], P(('doc', 'ctx')), parts along dimension 0, may hold values from -6 to 6
- step_embed: bfloat16 [32, 4096], P('doc', 'ctx'), parts along dimension 0, may hold values from -6 to 6
- w_query: bfloat16 [4096, 2048], P('ctx'), may hold values from -1 to 1
- w_key: bfloat16 [4096, 512], P('ctx'), may hold values from -4 to 4
- w_value: bfloat16 [4096, 512], P('ctx'), may hold values from -0.09375 to 0.09375
Outputs:
- context_out: bfloat16 [131072, 2048], P(('doc', 'ctx')), parts along dimension 0
- decoded: bfloat16 [32, 2048], P('doc'), parts along dimension 0
The draws below stay inside these ranges and needn't reach their ends.
There are 8 independent parts, one for each index of `doc`. The reference program is written for one: setup_inputs(seed, part) draws one part's arguments, and reference() takes and returns one part's arrays. A program takes and returns all parts, laid end to end along the dimension named above; an argument that names none is the same for every part. Nothing has to cross between parts.
All inputs are finite; a program needn't handle non-finite values.
Results may differ from the reference program's by a relative error of at most 0.008.
The reference program's roundings to bfloat16 on the way count: a program that leaves them out, or rounds other values in their place, can miss the bound.
Values may be sent and summed in bfloat16 or wider, within the bound.
No kernel may reach another device: no remote copies, remote signals or barrier semaphores. Data moves between devices by JAX's collectives and lax.ppermute only.
A program may use at most 64 MiB of HBM per device.

```python
import math
import jax
import jax.numpy as jnp
from jax import lax

D = 4096
HS = 128
HQ = 16
HK = 4
GROUP = 4
BLOCK = 256
STEPS = 4
SHARDS = 64
DOCLEN = 16384


def draw_projections(key):
    base = jnp.clip(jax.random.normal(jax.random.fold_in(key, 101), (D, HQ * HS), jnp.float32), -6.0, 6.0) * D ** (-0.5)
    noise = jnp.clip(jax.random.normal(jax.random.fold_in(key, 102), (D, HK * HS), jnp.float32), -6.0, 6.0) * (0.5 * D ** (-0.5))
    summed = base.reshape(D, HK, HQ // HK, HS).sum(axis=2).reshape(D, HK * HS)
    return (base, 1.2 * summed + noise)


def draw_w_query(key, part):
    return draw_projections(key)[0].astype(jnp.bfloat16)


def draw_w_key(key, part):
    return draw_projections(key)[1].astype(jnp.bfloat16)


def draw_ctx_key(key, part):
    total_rows = SHARDS * BLOCK
    width = HK * HS
    result = jnp.clip(jax.random.normal(jax.random.fold_in(key, 201), (total_rows, width), jnp.float32), -5.0, 5.0) * 3.0
    return result.astype(jnp.bfloat16)


def level_of(stream_key, shape, shards, smallest, largest):
    factor_of, own = 1.0, jax.random.fold_in(stream_key, 6)
    for axis_at, shards_of in shards:
        draws = jnp.exp(jax.random.uniform(jax.random.fold_in(own, axis_at), (shards_of,), jnp.float32, smallest / len(shards), largest / len(shards)))
        factor_of = factor_of * jnp.repeat(draws, shape[axis_at] // shards_of).reshape([-1 if axis == axis_at else 1 for axis in range(len(shape))])
    return factor_of


def centred(key, shape, deviation, reach, split=(), kind=jnp.bfloat16):
    loudness = level_of(key, shape, split, -0.22, 0.18) if split else 1.0
    drawn = jax.random.normal(key, shape, jnp.float32) * deviation * loudness
    return jnp.minimum(jnp.maximum(drawn, -reach), reach).astype(kind)


def setup_inputs(seed: int = 0, part: int = 0) -> dict:
    seeds = jax.random.split(jax.random.key(seed), 8)
    part_keys = jax.random.split(jax.random.fold_in(seeds[7], part), 8)
    return {
        "ctx_query": centred(part_keys[0], (DOCLEN, HQ * HS), 1.0, 6.0, ((0, 64),)),
        "ctx_key": draw_ctx_key(jax.random.fold_in(jax.random.fold_in(seeds[7], part), 71), part),
        "ctx_value": centred(part_keys[2], (DOCLEN, HK * HS), 1.0, 6.0, ((0, 64),)),
        "step_embed": centred(part_keys[3], (STEPS, D), 1.0, 6.0, ((1, 64),)),
        "w_query": draw_w_query(jax.random.fold_in(seeds[7], 71), part),
        "w_key": draw_w_key(jax.random.fold_in(seeds[7], 71), part),
        "w_value": centred(seeds[6], (D, HK * HS), D ** -0.5, 0.09375, ((0, 64),)),
    }


def rotate(values, positions):
    half_width = values.shape[-1] // 2
    frequency = jnp.exp(jnp.arange(half_width, dtype=jnp.float32) * (-2.0 * math.log(500000.0) / values.shape[-1]))
    angles = positions[:, None] * frequency[None, :]
    cosine = jnp.cos(angles)[:, None, :]
    sine = jnp.sin(angles)[:, None, :]
    first_half = values[..., :half_width]
    second_half = values[..., half_width:]
    return jnp.concatenate([first_half * cosine - second_half * sine, second_half * cosine + first_half * sine], axis=-1)

def rounded(values):
    return lax.optimization_barrier(values.astype(jnp.bfloat16)).astype(jnp.float32)

def reference(ctx_query, ctx_key, ctx_value, step_embed, w_query, w_key, w_value):
    score_scale = 1.0 / math.sqrt(HS)
    queries = ctx_query.reshape(SHARDS, BLOCK, HK, GROUP, HS)
    keys = ctx_key.reshape(SHARDS, BLOCK, HK, HS)
    values = ctx_value.reshape(SHARDS, BLOCK, HK, HS)
    anchor_key = keys[0].astype(jnp.float32)
    anchor_value = values[0].astype(jnp.float32)
    causal = jnp.arange(BLOCK)[:, None] >= jnp.arange(BLOCK)[None, :]

    def shard_attention(packed):
        shard_query, shard_key, shard_value, shard_index = packed
        query_float = shard_query.astype(jnp.float32)
        own_scores = jnp.einsum('ihgd,jhd->hgij', query_float, shard_key.astype(jnp.float32)) * score_scale
        own_scores = jnp.where(causal, own_scores, -jnp.inf)
        anchor_scores = jnp.einsum('ihgd,jhd->hgij', query_float, anchor_key) * score_scale
        anchor_scores = jnp.where(shard_index != 0, anchor_scores, -jnp.inf)
        row_max = jnp.maximum(lax.optimization_barrier(jnp.max(own_scores, axis=-1)), lax.optimization_barrier(jnp.max(anchor_scores, axis=-1)))
        own_weights = jnp.exp(own_scores - row_max[..., None])
        anchor_weights = jnp.exp(anchor_scores - row_max[..., None])
        row_sum = lax.optimization_barrier(jnp.sum(own_weights, axis=-1)) + lax.optimization_barrier(jnp.sum(anchor_weights, axis=-1))
        weighted = jnp.einsum('hgij,jhd->ihgd', rounded(own_weights), shard_value.astype(jnp.float32))
        weighted = weighted + jnp.einsum('hgij,jhd->ihgd', rounded(anchor_weights), anchor_value)
        return (weighted / jnp.transpose(row_sum, (2, 0, 1))[..., None]).astype(jnp.bfloat16)
    context_out = lax.map(shard_attention, (queries, keys, values, jnp.arange(SHARDS, dtype=jnp.int32)))
    context_out = context_out.reshape(SHARDS * BLOCK, HQ * HS)
    query_new = jnp.dot(step_embed, w_query, preferred_element_type=jnp.float32).reshape(STEPS, HQ, HS)
    key_new = jnp.dot(step_embed, w_key, preferred_element_type=jnp.float32).reshape(STEPS, HK, HS)
    value_new = jnp.dot(step_embed, w_value, preferred_element_type=jnp.float32).reshape(STEPS, HK, HS)
    positions = (SHARDS * BLOCK + jnp.arange(STEPS)).astype(jnp.float32)
    query_new = rounded(rotate(query_new, positions)).reshape(STEPS, HK, GROUP, HS)
    key_new = rounded(rotate(key_new, positions))
    value_new = rounded(value_new)
    cache_scores = jnp.einsum('shgd,cjhd->shgcj', query_new, keys.astype(jnp.float32)) * score_scale
    shard_max = lax.optimization_barrier(jnp.max(cache_scores, axis=-1))
    cache_weights = jnp.exp(cache_scores - shard_max[..., None])
    shard_sum = lax.optimization_barrier(jnp.sum(cache_weights, axis=-1))
    shard_out = jnp.einsum('shgcj,cjhd->shgcd', rounded(cache_weights), values.astype(jnp.float32))
    new_scores = jnp.einsum('shgd,thd->shgt', query_new, key_new) * score_scale
    visible = jnp.arange(STEPS)[:, None, None, None] >= jnp.arange(STEPS)[None, None, None, :]
    new_scores = jnp.where(visible, new_scores, -jnp.inf)
    new_max = lax.optimization_barrier(jnp.max(new_scores, axis=-1))
    new_weights = jnp.exp(new_scores - new_max[..., None])
    new_sum = lax.optimization_barrier(jnp.sum(new_weights, axis=-1))
    new_out = jnp.einsum('shgt,thd->shgd', rounded(new_weights), value_new)
    global_max = jnp.maximum(lax.optimization_barrier(jnp.max(shard_max, axis=-1)), new_max)
    shard_factor = jnp.exp(shard_max - global_max[..., None])
    new_factor = jnp.exp(new_max - global_max)
    total_sum = lax.optimization_barrier(jnp.sum(shard_sum * shard_factor, axis=-1)) + new_sum * new_factor
    total_out = lax.optimization_barrier(jnp.sum(shard_out * shard_factor[..., None], axis=3)) + new_out * new_factor[..., None]
    decoded = (total_out / total_sum[..., None]).reshape(STEPS, HQ * HS).astype(jnp.bfloat16)
    return (context_out, decoded)
```

```python
import functools
import math

import jax
import jax.numpy as jnp
from jax import lax
from jax.experimental import pallas as pl
from jax.experimental.pallas import tpu as pltpu
from jax.sharding import Mesh
from jax.sharding import PartitionSpec as P

HS = 128
HQ = 16
HK = 4
GROUP = 4
STEPS = 4
QROWS = GROUP * STEPS
PROWS = QROWS + 2 * STEPS
SCALE = 1.0 / math.sqrt(HS)
EXP2_SCALE = SCALE * math.log2(math.e)
BF16 = jnp.bfloat16
F32 = jnp.float32
INTERPRET = False


def dot(a, b):
    return lax.dot_general(a, b, (((1,), (0,)), ((), ())), preferred_element_type=F32)


def dot_t(a, b):
    return lax.dot_general(a, b, (((1,), (1,)), ((), ())), preferred_element_type=F32)


def split2(value):
    high = value.astype(BF16)
    return high, (value - high.astype(F32)).astype(BF16)


def split3(value):
    high = value.astype(BF16)
    rest = value - high.astype(F32)
    middle = rest.astype(BF16)
    return high, middle, (rest - middle.astype(F32)).astype(BF16)


def project_kernel(embed_ref, wq_ref, wk_ref, wv_ref, key_ref, value_ref, out_ref):
    block = key_ref.shape[0]
    pick = (
        lax.broadcasted_iota(jnp.int32, (PROWS, STEPS), 0) % STEPS
        == lax.broadcasted_iota(jnp.int32, (PROWS, STEPS), 1)
    )
    repeated = dot(pick.astype(BF16), embed_ref[...]).astype(BF16)
    row_head = lax.broadcasted_iota(jnp.int32, repeated.shape, 0) // STEPS
    placed = [jnp.where(row_head == j, repeated, 0).astype(BF16) for j in range(GROUP + 2)]
    for group in range(HK):
        cols = slice(group * HS, (group + 1) * HS)
        part = dot(placed[GROUP], wk_ref[:, cols]) + dot(placed[GROUP + 1], wv_ref[:, cols])
        for j in range(GROUP):
            head = group * GROUP + j
            part = part + dot(placed[j], wq_ref[:, head * HS : (head + 1) * HS])
        high, low = split2(part)
        out_ref[group, 0:PROWS] = high
        out_ref[group, PROWS : 2 * PROWS] = low
        out_ref[group, 2 * PROWS : 2 * PROWS + block] = key_ref[:, cols]
        out_ref[group, 2 * PROWS + block : 2 * PROWS + 2 * block] = value_ref[:, cols]


def spread_kernel(in_ref, out_ref):
    sources = in_ref.shape[0]
    peers = out_ref.shape[0]
    piece = (in_ref.shape[1] - 2 * PROWS) // peers
    total = in_ref[0, 0:PROWS].astype(F32) + in_ref[0, PROWS : 2 * PROWS].astype(F32)
    for source in range(1, sources):
        total = total + (
            in_ref[source, 0:PROWS].astype(F32) + in_ref[source, PROWS : 2 * PROWS].astype(F32)
        )
    high, low = split2(total)
    for peer in range(peers):
        out_ref[peer, 0:PROWS] = high
        out_ref[peer, PROWS : 2 * PROWS] = low
        start = 2 * PROWS + peer * piece
        out_ref[peer, 2 * PROWS : 2 * PROWS + piece] = in_ref[0, start : start + piece]


def decode_kernel(sums_ref, cache_ref, cos_ref, sin_ref, out_ref, new_ref):
    peers = sums_ref.shape[0]
    blocks = cache_ref.shape[0]
    block = (cache_ref.shape[1] - 2 * PROWS) // 2
    piece = sums_ref.shape[1] - 2 * PROWS
    total = sums_ref[0, 0:PROWS].astype(F32) + sums_ref[0, PROWS : 2 * PROWS].astype(F32)
    for peer in range(1, peers):
        total = total + (
            sums_ref[peer, 0:PROWS].astype(F32) + sums_ref[peer, PROWS : 2 * PROWS].astype(F32)
        )
    rotated = total * cos_ref[...] + pltpu.roll(total, HS // 2, 1) * sin_ref[...]
    query = rotated[0:QROWS].astype(BF16)
    parts = []
    for c in range(blocks):
        keys = cache_ref[c, 2 * PROWS : 2 * PROWS + block]
        values = cache_ref[c, 2 * PROWS + block : 2 * PROWS + 2 * block]
        scores = dot_t(query, keys) * SCALE
        part_max = jnp.max(scores, axis=1, keepdims=True)
        weights = jnp.exp(scores - part_max)
        part_sum = jnp.sum(weights, axis=1, keepdims=True)
        parts.append((part_max, part_sum, dot(weights.astype(BF16), values)))
    joint_max = functools.reduce(jnp.maximum, [part[0] for part in parts])
    joint_sum, joint_out = 0.0, 0.0
    for part_max, part_sum, part_out in parts:
        factor = jnp.exp(part_max - joint_max)
        joint_sum = joint_sum + part_sum * factor
        joint_out = joint_out + part_out * factor
    lane = lax.broadcasted_iota(jnp.int32, (QROWS, HS), 1)
    stats = jnp.zeros((QROWS, HS), F32)
    for at, value in enumerate(split3(joint_max) + split3(joint_sum)):
        stats = jnp.where(lane == at, value.astype(F32), stats)
    stats = stats.astype(BF16)
    high, low = split2(joint_out)
    anchor = sums_ref[0, 2 * PROWS : 2 * PROWS + piece]
    for peer in range(peers):
        out_ref[peer, 0:QROWS] = high
        out_ref[peer, QROWS : 2 * QROWS] = low
        out_ref[peer, 2 * QROWS : 3 * QROWS] = stats
        out_ref[peer, 3 * QROWS : 3 * QROWS + piece] = anchor
    key_new = rotated[QROWS:PROWS].astype(BF16)
    value_new = pltpu.roll(total[QROWS:PROWS], STEPS, 0).astype(BF16)
    scores = dot_t(query, key_new) * SCALE
    step = lax.broadcasted_iota(jnp.int32, scores.shape, 0) % STEPS
    later = lax.broadcasted_iota(jnp.int32, scores.shape, 1)
    scores = jnp.where(later <= step, scores, -jnp.inf)
    new_max = jnp.max(scores, axis=1, keepdims=True)
    weights = jnp.exp(scores - new_max)
    new_sum = jnp.sum(weights, axis=1, keepdims=True)
    new_ref[0] = jnp.broadcast_to(new_max, (QROWS, HS))
    new_ref[1] = jnp.broadcast_to(new_sum, (QROWS, HS))
    new_ref[2] = dot(weights.astype(BF16), value_new)


def combine_kernel(parts_ref, new_ref, out_ref):
    peers = parts_ref.shape[0]
    piece = parts_ref.shape[1] - 3 * QROWS
    maxima, sums, outs = [], [], []
    for peer in range(peers):
        stats = parts_ref[peer, 2 * QROWS : 3 * QROWS].astype(F32)
        maxima.append(stats[:, 0:1] + stats[:, 1:2] + stats[:, 2:3])
        sums.append(stats[:, 3:4] + stats[:, 4:5] + stats[:, 5:6])
    new_max = new_ref[0][:, 0:1]
    global_max = functools.reduce(jnp.maximum, maxima + [new_max])
    factor = jnp.exp(new_max - global_max)
    total_sum = new_ref[1][:, 0:1] * factor
    total_out = new_ref[2] * factor
    for peer in range(peers):
        factor = jnp.exp(maxima[peer] - global_max)
        part_out = parts_ref[peer, 0:QROWS].astype(F32) + parts_ref[peer, QROWS : 2 * QROWS].astype(F32)
        total_sum = total_sum + sums[peer] * factor
        total_out = total_out + part_out * factor
    decoded = (total_out / total_sum).astype(BF16)
    for x in range(out_ref.shape[0]):
        out_ref[x, 0:QROWS] = decoded
        for peer in range(peers):
            start = QROWS + peer * piece
            out_ref[x, start : start + piece] = parts_ref[peer, 3 * QROWS : 3 * QROWS + piece]


def prefill_kernel(query_ref, key_ref, value_ref, anchor_ref, out_ref, decoded_ref):
    block = key_ref.shape[0]
    half = block // 2
    use_anchor = (lax.axis_index("x") + lax.axis_index("z")) != 0
    anchor_key = anchor_ref[0, QROWS : QROWS + block]
    anchor_value = anchor_ref[0, QROWS + block : QROWS + 2 * block]
    causal = lax.broadcasted_iota(jnp.int32, (half, half), 0) >= lax.broadcasted_iota(
        jnp.int32, (half, half), 1
    )
    for j in range(GROUP):
        cols = slice(j * HS, (j + 1) * HS)
        for part in range(2):
            rows = slice(part * half, (part + 1) * half)
            seen = (part + 1) * half
            query = query_ref[rows, cols]
            own = dot_t(query, key_ref[0:seen, :])
            diagonal = jnp.where(causal, own[:, part * half :], -jnp.inf)
            own = diagonal if part == 0 else jnp.concatenate([own[:, :half], diagonal], axis=1)
            anchor = dot_t(query, anchor_key)
            own_max = jnp.max(own, axis=1, keepdims=True)
            anchor_max = jnp.max(anchor, axis=1, keepdims=True)
            row_max = jnp.where(use_anchor, jnp.maximum(own_max, anchor_max), own_max)
            own_weights = jnp.exp2((own - row_max) * EXP2_SCALE)
            anchor_shift = jnp.where(use_anchor, row_max, jnp.inf)
            anchor_weights = jnp.exp2((anchor - anchor_shift) * EXP2_SCALE)
            row_sum = jnp.sum(own_weights, axis=1, keepdims=True) + jnp.sum(
                anchor_weights, axis=1, keepdims=True
            )
            weighted = dot(own_weights.astype(BF16), value_ref[0:seen, :]) + dot(
                anchor_weights.astype(BF16), anchor_value
            )
            out_ref[rows, cols] = (weighted / row_sum).astype(BF16)
        pick = (
            lax.broadcasted_iota(jnp.int32, (STEPS, QROWS), 1)
            == lax.broadcasted_iota(jnp.int32, (STEPS, QROWS), 0) + j * STEPS
        )
        decoded_ref[:, cols] = dot(pick.astype(BF16), anchor_ref[0, 0:QROWS]).astype(BF16)


def rotary_tables(position, step_count):
    half_width = HS // 2
    frequency = jnp.exp(
        jnp.arange(half_width, dtype=F32) * (-2.0 * math.log(500000.0) / HS)
    )
    positions = (position + jnp.arange(step_count)).astype(F32)
    angles = positions[:, None] * frequency[None, :]
    cosine, sine = jnp.cos(angles), jnp.sin(angles)
    cosine = jnp.concatenate([cosine, cosine], axis=1)
    sine = jnp.concatenate([-sine, sine], axis=1)
    return jnp.tile(cosine, (GROUP + 2, 1)), jnp.tile(sine, (GROUP + 2, 1))


def call(kernel, out_shape, **kwargs):
    return pl.pallas_call(kernel, out_shape=out_shape, interpret=INTERPRET, **kwargs)


def on_device(ctx_query, ctx_key, ctx_value, step_embed, w_query, w_key, w_value):
    block = ctx_query.shape[0]
    nx, nz = lax.axis_size("x"), lax.axis_size("z")
    piece = 2 * block // nz
    shape = jax.ShapeDtypeStruct
    cosine, sine = rotary_tables(nx * nz * block, STEPS)

    slabs = call(project_kernel, shape((nx, 2 * PROWS + 2 * block, HS), BF16), name="project")(
        step_embed, w_query, w_key, w_value, ctx_key, ctx_value
    )
    cache = lax.all_to_all(slabs, "x", 0, 0, tiled=True)
    spread = call(spread_kernel, shape((nz, 2 * PROWS + piece, HS), BF16), name="spread")(cache)
    sums = lax.all_to_all(spread, "z", 0, 0, tiled=True)
    parts, new = call(
        decode_kernel,
        (shape((nz, 3 * QROWS + piece, HS), BF16), shape((3, QROWS, HS), F32)),
        name="decode",
    )(sums, cache, cosine, sine)
    parts = lax.all_to_all(parts, "z", 0, 0, tiled=True)
    heads = call(combine_kernel, shape((nx, QROWS + 2 * block, HS), BF16), name="combine")(parts, new)
    heads = lax.all_to_all(heads, "x", 0, 0, tiled=True)
    width = GROUP * HS
    context_out, decoded = call(
        prefill_kernel,
        (shape((block, HQ * HS), BF16), shape((STEPS, HQ * HS), BF16)),
        name="prefill",
        grid=(HK,),
        in_specs=[
            pl.BlockSpec((block, width), lambda h: (0, h)),
            pl.BlockSpec((block, HS), lambda h: (0, h)),
            pl.BlockSpec((block, HS), lambda h: (0, h)),
            pl.BlockSpec((1, QROWS + 2 * block, HS), lambda h: (h, 0, 0)),
        ],
        out_specs=[
            pl.BlockSpec((block, width), lambda h: (0, h)),
            pl.BlockSpec((STEPS, width), lambda h: (0, h)),
        ],
    )(ctx_query, ctx_key, ctx_value, heads)
    return context_out, decoded


def solution(mesh):
    docs, contexts = mesh.shape["doc"], mesh.shape["ctx"]
    split = Mesh(mesh.devices.reshape(docs, HK, contexts // HK), ("doc", "x", "z"))
    ctx = ("x", "z")
    rows = P(("doc",) + ctx, None)
    return jax.shard_map(
        on_device,
        mesh=split,
        in_specs=(rows, rows, rows, P("doc", ctx), P(ctx, None), P(ctx, None), P(ctx, None)),
        out_specs=(rows, P("doc", None)),
        check_vma=False,
    )
```

```python
import functools
import math

import jax
import jax.numpy as jnp
from jax import lax
from jax.experimental import pallas as pl
from jax.experimental.pallas import tpu as pltpu
from jax.sharding import Mesh
from jax.sharding import PartitionSpec as P

HS = 128
HQ = 16
HK = 4
GROUP = 4
STEPS = 4
QROWS = GROUP * STEPS
PROWS = QROWS + 2 * STEPS
SROWS = QROWS // 2
SCALE = 1.0 / math.sqrt(HS)
EXP2_SCALE = SCALE * math.log2(math.e)
BF16 = jnp.bfloat16
F32 = jnp.float32
INTERPRET = False


def dot(a, b):
    return lax.dot_general(a, b, (((1,), (0,)), ((), ())), preferred_element_type=F32)


def dot_t(a, b):
    return lax.dot_general(a, b, (((1,), (1,)), ((), ())), preferred_element_type=F32)


def split2(value):
    high = value.astype(BF16)
    return high, (value - high.astype(F32)).astype(BF16)


def split3(value):
    high = value.astype(BF16)
    rest = value - high.astype(F32)
    middle = rest.astype(BF16)
    return high, middle, (rest - middle.astype(F32)).astype(BF16)


def project_kernel(embed_ref, wq_ref, wk_ref, wv_ref, key_ref, value_ref, out_ref, part_ref):
    block = key_ref.shape[0]
    embed = embed_ref[...]
    query, key, value = dot(embed, wq_ref[...]), dot(embed, wk_ref[...]), dot(embed, wv_ref[...])
    for group in range(HK):
        cols = slice(group * HS, (group + 1) * HS)
        for j in range(GROUP):
            head = group * GROUP + j
            part_ref[group, j * STEPS : (j + 1) * STEPS] = query[:, head * HS : (head + 1) * HS]
        part_ref[group, QROWS : QROWS + STEPS] = key[:, cols]
        part_ref[group, QROWS + STEPS : PROWS] = value[:, cols]
        out_ref[group, 2 * PROWS : 2 * PROWS + block] = key_ref[:, cols]
        out_ref[group, 2 * PROWS + block : 2 * PROWS + 2 * block] = value_ref[:, cols]
    for group in range(HK):
        high, low = split2(part_ref[group])
        out_ref[group, 0:PROWS] = high
        out_ref[group, PROWS : 2 * PROWS] = low


def spread_kernel(in_ref, out_ref):
    sources = in_ref.shape[0]
    peers = out_ref.shape[0]
    piece = (in_ref.shape[1] - 2 * PROWS) // peers
    total = in_ref[0, 0:PROWS].astype(F32) + in_ref[0, PROWS : 2 * PROWS].astype(F32)
    for source in range(1, sources):
        total = total + (
            in_ref[source, 0:PROWS].astype(F32) + in_ref[source, PROWS : 2 * PROWS].astype(F32)
        )
    high, low = split2(total)
    for peer in range(peers):
        out_ref[peer, 0:PROWS] = high
        out_ref[peer, PROWS : 2 * PROWS] = low
        start = 2 * PROWS + peer * piece
        out_ref[peer, 2 * PROWS : 2 * PROWS + piece] = in_ref[0, start : start + piece]


def decode_kernel(sums_ref, cache_ref, cos_ref, sin_ref, out_ref, new_ref):
    peers = sums_ref.shape[0]
    blocks = cache_ref.shape[0]
    block = (cache_ref.shape[1] - 2 * PROWS) // 2
    piece = sums_ref.shape[1] - 2 * PROWS
    total = sums_ref[0, 0:PROWS].astype(F32) + sums_ref[0, PROWS : 2 * PROWS].astype(F32)
    for peer in range(1, peers):
        total = total + (
            sums_ref[peer, 0:PROWS].astype(F32) + sums_ref[peer, PROWS : 2 * PROWS].astype(F32)
        )
    rotated = total * cos_ref[...] + pltpu.roll(total, HS // 2, 1) * sin_ref[...]
    query = rotated[0:QROWS].astype(BF16)
    parts = []
    for c in range(blocks):
        keys = cache_ref[c, 2 * PROWS : 2 * PROWS + block]
        values = cache_ref[c, 2 * PROWS + block : 2 * PROWS + 2 * block]
        scores = dot_t(query, keys) * SCALE
        part_max = jnp.max(scores, axis=1, keepdims=True)
        weights = jnp.exp(scores - part_max)
        part_sum = jnp.sum(weights, axis=1, keepdims=True)
        parts.append((part_max, part_sum, dot(weights.astype(BF16), values)))
    joint_max = functools.reduce(jnp.maximum, [part[0] for part in parts])
    joint_sum, joint_out = 0.0, 0.0
    for part_max, part_sum, part_out in parts:
        factor = jnp.exp(part_max - joint_max)
        joint_sum = joint_sum + part_sum * factor
        joint_out = joint_out + part_out * factor
    lane = lax.broadcasted_iota(jnp.int32, (QROWS, HS), 1)
    stats = jnp.zeros((QROWS, HS), F32)
    for at, value in enumerate(split3(joint_max) + split3(joint_sum)):
        stats = jnp.where(lane == at, value.astype(F32), stats)
    stats = jnp.where(lane[:SROWS] < HS // 2, stats[:SROWS], pltpu.roll(stats[SROWS:], HS // 2, 1))
    stats = stats.astype(BF16)
    joint_out = joint_out.astype(BF16)
    anchor = sums_ref[0, 2 * PROWS : 2 * PROWS + piece]
    for peer in range(peers):
        out_ref[peer, 0:QROWS] = joint_out
        out_ref[peer, QROWS : QROWS + SROWS] = stats
        out_ref[peer, QROWS + SROWS : QROWS + SROWS + piece] = anchor
    key_new = rotated[QROWS:PROWS].astype(BF16)
    value_new = pltpu.roll(total[QROWS:PROWS], STEPS, 0).astype(BF16)
    scores = dot_t(query, key_new) * SCALE
    step = lax.broadcasted_iota(jnp.int32, scores.shape, 0) % STEPS
    later = lax.broadcasted_iota(jnp.int32, scores.shape, 1)
    scores = jnp.where(later <= step, scores, -jnp.inf)
    new_max = jnp.max(scores, axis=1, keepdims=True)
    weights = jnp.exp(scores - new_max)
    new_sum = jnp.sum(weights, axis=1, keepdims=True)
    new_ref[0] = jnp.broadcast_to(new_max, (QROWS, HS))
    new_ref[1] = jnp.broadcast_to(new_sum, (QROWS, HS))
    new_ref[2] = dot(weights.astype(BF16), value_new)


def combine_kernel(parts_ref, new_ref, out_ref):
    peers = parts_ref.shape[0]
    first = QROWS + SROWS
    piece = parts_ref.shape[1] - first
    maxima, sums = [], []
    for peer in range(peers):
        stats = parts_ref[peer, QROWS:first].astype(F32)
        stats = jnp.concatenate([stats, pltpu.roll(stats, HS // 2, 1)], axis=0)
        maxima.append(stats[:, 0:1] + stats[:, 1:2] + stats[:, 2:3])
        sums.append(stats[:, 3:4] + stats[:, 4:5] + stats[:, 5:6])
    new_max = new_ref[0][:, 0:1]
    global_max = functools.reduce(jnp.maximum, maxima + [new_max])
    factor = jnp.exp(new_max - global_max)
    total_sum = new_ref[1][:, 0:1] * factor
    total_out = new_ref[2] * factor
    for peer in range(peers):
        factor = jnp.exp(maxima[peer] - global_max)
        total_sum = total_sum + sums[peer] * factor
        total_out = total_out + parts_ref[peer, 0:QROWS].astype(F32) * factor
    decoded = (total_out / total_sum).astype(BF16)
    for x in range(out_ref.shape[0]):
        out_ref[x, 0:QROWS] = decoded
        for peer in range(peers):
            start = QROWS + peer * piece
            out_ref[x, start : start + piece] = parts_ref[peer, first : first + piece]


def prefill_kernel(query_ref, key_ref, value_ref, anchor_ref, out_ref, decoded_ref):
    block = key_ref.shape[0]
    half = block // 2
    group = pl.program_id(0)
    use_anchor = (lax.axis_index("x") + lax.axis_index("z")) != 0
    head_cols = pl.ds(pl.multiple_of(group * HS, HS), HS)
    key = key_ref[:, head_cols]
    anchor_key = anchor_ref[group, QROWS : QROWS + block]
    anchor_value = anchor_ref[group, QROWS + block : QROWS + 2 * block]
    values = jnp.concatenate([anchor_value.T, value_ref[:, head_cols].T], axis=1)
    causal = lax.broadcasted_iota(jnp.int32, (half, half), 0) <= lax.broadcasted_iota(
        jnp.int32, (half, half), 1
    )
    for j in range(GROUP):
        cols = slice(j * HS, (j + 1) * HS)
        query = query_ref[:, pl.ds(pl.multiple_of((group * GROUP + j) * HS, HS), HS)]
        anchor_scores = dot_t(anchor_key, query)
        early_scores = dot_t(key[:half], query)
        late_scores = dot_t(key[half:], query[half:])
        for part in range(2):
            rows = slice(part * half, (part + 1) * half)
            anchor = anchor_scores[:, rows]
            if part == 0:
                own = jnp.where(causal, early_scores[:, rows], -jnp.inf)
            else:
                own = jnp.concatenate(
                    [early_scores[:, rows], jnp.where(causal, late_scores, -jnp.inf)], axis=0
                )
            own_max = jnp.max(own, axis=0, keepdims=True)
            anchor_max = jnp.max(anchor, axis=0, keepdims=True)
            row_max = jnp.where(use_anchor, jnp.maximum(own_max, anchor_max), own_max)
            anchor_shift = jnp.where(use_anchor, row_max, jnp.inf)
            own_weights = jnp.exp2((own - row_max) * EXP2_SCALE)
            anchor_weights = jnp.exp2((anchor - anchor_shift) * EXP2_SCALE)
            row_sum = jnp.sum(own_weights, axis=0, keepdims=True) + jnp.sum(
                anchor_weights, axis=0, keepdims=True
            )
            weights = jnp.concatenate(
                [anchor_weights.astype(BF16), own_weights.astype(BF16)], axis=0
            )
            weighted = dot(values[:, : block + (part + 1) * half], weights)
            out_ref[rows, cols] = (weighted * (1.0 / row_sum)).T.astype(BF16)
        pick = (
            lax.broadcasted_iota(jnp.int32, (STEPS, QROWS), 1)
            == lax.broadcasted_iota(jnp.int32, (STEPS, QROWS), 0) + j * STEPS
        )
        decoded_ref[:, cols] = dot(pick.astype(BF16), anchor_ref[group, 0:QROWS]).astype(BF16)


def rotary_tables(position):
    shape = (PROWS, HS)
    lane = lax.broadcasted_iota(jnp.int32, shape, 1)
    step = lax.broadcasted_iota(jnp.int32, shape, 0) % STEPS
    half_width = HS // 2
    frequency = jnp.exp((lane % half_width).astype(F32) * (-2.0 * math.log(500000.0) / HS))
    angles = (position + step).astype(F32) * frequency
    sine = jnp.sin(angles)
    return jnp.cos(angles), jnp.where(lane < half_width, -sine, sine)


VMEM_SPEC = pl.BlockSpec(memory_space=pltpu.VMEM)


def in_vmem(value):
    return value if INTERPRET else pltpu.with_memory_space_constraint(value, pltpu.VMEM)


def call(kernel, out_shape, **kwargs):
    if not INTERPRET:
        out_shape = jax.tree.map(lambda out: pltpu.VMEM(out.shape, out.dtype), out_shape)
    return pl.pallas_call(
        kernel,
        out_shape=out_shape,
        out_specs=jax.tree.map(lambda _: VMEM_SPEC, out_shape),
        interpret=INTERPRET,
        **kwargs,
    )


def on_device(ctx_query, ctx_key, ctx_value, step_embed, w_query, w_key, w_value):
    block = ctx_query.shape[0]
    nx, nz = lax.axis_size("x"), lax.axis_size("z")
    piece = 2 * block // nz
    shape = jax.ShapeDtypeStruct
    cosine, sine = rotary_tables(nx * nz * block)

    slabs = call(
        project_kernel,
        shape((nx, 2 * PROWS + 2 * block, HS), BF16),
        name="project",
        scratch_shapes=[pltpu.VMEM((HK, PROWS, HS), F32)],
    )(step_embed, w_query, w_key, w_value, ctx_key, ctx_value)
    cache = in_vmem(lax.all_to_all(slabs, "x", 0, 0, tiled=True))
    spread = call(
        spread_kernel,
        shape((nz, 2 * PROWS + piece, HS), BF16),
        name="spread",
        in_specs=[VMEM_SPEC],
    )(cache)
    sums = in_vmem(lax.all_to_all(spread, "z", 0, 0, tiled=True))
    parts, new = call(
        decode_kernel,
        (shape((nz, QROWS + SROWS + piece, HS), BF16), shape((3, QROWS, HS), F32)),
        name="decode",
        in_specs=[VMEM_SPEC] * 4,
    )(sums, cache, in_vmem(cosine), in_vmem(sine))
    parts = in_vmem(lax.all_to_all(parts, "z", 0, 0, tiled=True))
    heads = call(
        combine_kernel,
        shape((nx, QROWS + 2 * block, HS), BF16),
        name="combine",
        in_specs=[VMEM_SPEC] * 2,
    )(parts, in_vmem(new))
    heads = in_vmem(lax.all_to_all(heads, "x", 0, 0, tiled=True))
    width = GROUP * HS
    context_out, decoded = pl.pallas_call(
        prefill_kernel,
        out_shape=(shape((block, HQ * HS), BF16), shape((STEPS, HQ * HS), BF16)),
        name="prefill",
        grid=(HK,),
        in_specs=[VMEM_SPEC] * 4,
        out_specs=[
            pl.BlockSpec((block, width), lambda h: (0, h)),
            pl.BlockSpec((STEPS, width), lambda h: (0, h)),
        ],
        interpret=INTERPRET,
    )(in_vmem(ctx_query), in_vmem(ctx_key), in_vmem(ctx_value), heads)
    return context_out, decoded


def solution(mesh):
    docs, contexts = mesh.shape["doc"], mesh.shape["ctx"]
    split = Mesh(mesh.devices.reshape(docs, HK, contexts // HK), ("doc", "x", "z"))
    ctx = ("x", "z")
    rows = P(("doc",) + ctx, None)
    return jax.shard_map(
        on_device,
        mesh=split,
        in_specs=(rows, rows, rows, P("doc", ctx), P(ctx, None), P(ctx, None), P(ctx, None)),
        out_specs=(rows, P("doc", None)),
        check_vma=False,
    )
```

```python
import functools
import math

import jax
import jax.numpy as jnp
from jax import lax
from jax.experimental import pallas as pl
from jax.experimental.pallas import tpu as pltpu
from jax.sharding import Mesh
from jax.sharding import PartitionSpec as P

HS = 128
HQ = 16
HK = 4
GROUP = 4
STEPS = 4
QROWS = GROUP * STEPS
PROWS = QROWS + 2 * STEPS
SROWS = QROWS // 2
HROWS = 2 * QROWS + SROWS
SCALE = 1.0 / math.sqrt(HS)
EXP2_SCALE = SCALE * math.log2(math.e)
BF16 = jnp.bfloat16
F32 = jnp.float32
INTERPRET = False


def dot(a, b):
    return lax.dot_general(a, b, (((1,), (0,)), ((), ())), preferred_element_type=F32)


def dot_t(a, b):
    return lax.dot_general(a, b, (((1,), (1,)), ((), ())), preferred_element_type=F32)


def split2(value):
    high = value.astype(BF16)
    return high, (value - high.astype(F32)).astype(BF16)


def split3(value):
    high = value.astype(BF16)
    rest = value - high.astype(F32)
    middle = rest.astype(BF16)
    return high, middle, (rest - middle.astype(F32)).astype(BF16)


def project_kernel(embed_ref, wq_ref, wk_ref, wv_ref, key_ref, value_ref, out_ref, part_ref):
    parities = out_ref.shape[0] // HK
    half = key_ref.shape[0] // parities
    embed = embed_ref[...]
    query, key, value = dot(embed, wq_ref[...]), dot(embed, wk_ref[...]), dot(embed, wv_ref[...])
    for group in range(HK):
        cols = slice(group * HS, (group + 1) * HS)
        for j in range(GROUP):
            head = group * GROUP + j
            part_ref[group, j * STEPS : (j + 1) * STEPS] = query[:, head * HS : (head + 1) * HS]
        part_ref[group, QROWS : QROWS + STEPS] = key[:, cols]
        part_ref[group, QROWS + STEPS : PROWS] = value[:, cols]
        for parity in range(parities):
            near = group * parities + parity
            rows = slice(parity * half, (parity + 1) * half)
            out_ref[near, 2 * PROWS : 2 * PROWS + half] = key_ref[rows, cols]
            out_ref[near, 2 * PROWS + half : 2 * PROWS + 2 * half] = value_ref[rows, cols]
    for group in range(HK):
        high, low = split2(part_ref[group])
        for parity in range(parities):
            out_ref[group * parities + parity, 0:PROWS] = high
            out_ref[group * parities + parity, PROWS : 2 * PROWS] = low


def add_projections(in_ref):
    total = in_ref[0, 0:PROWS].astype(F32) + in_ref[0, PROWS : 2 * PROWS].astype(F32)
    for source in range(1, in_ref.shape[0]):
        total = total + (
            in_ref[source, 0:PROWS].astype(F32) + in_ref[source, PROWS : 2 * PROWS].astype(F32)
        )
    return total


def spread_kernel(in_ref, out_ref):
    peers = out_ref.shape[0]
    piece = out_ref.shape[1] - 2 * PROWS
    high, low = split2(add_projections(in_ref))
    for peer in range(peers):
        out_ref[peer, 0:PROWS] = high
        out_ref[peer, PROWS : 2 * PROWS] = low
        start = 2 * PROWS + peer * piece
        out_ref[peer, 2 * PROWS : 2 * PROWS + piece] = in_ref[0, start : start + piece]


def pack_stats(part_max, part_sum):
    lane = lax.broadcasted_iota(jnp.int32, (QROWS, HS), 1)
    stats = jnp.zeros((QROWS, HS), F32)
    for at, value in enumerate(split3(part_max) + split3(part_sum)):
        stats = jnp.where(lane == at, value.astype(F32), stats)
    stats = jnp.where(lane[:SROWS] < HS // 2, stats[:SROWS], pltpu.roll(stats[SROWS:], HS // 2, 1))
    return stats.astype(BF16)


def unpack_stats(stats):
    stats = stats.astype(F32)
    stats = jnp.concatenate([stats, pltpu.roll(stats, HS // 2, 1)], axis=0)
    return (
        stats[:, 0:1] + stats[:, 1:2] + stats[:, 2:3],
        stats[:, 3:4] + stats[:, 4:5] + stats[:, 5:6],
    )


def join(parts):
    joint_max = functools.reduce(jnp.maximum, [part[0] for part in parts])
    joint_sum, joint_out = 0.0, 0.0
    for part_max, part_sum, part_out in parts:
        factor = jnp.exp(part_max - joint_max)
        joint_sum = joint_sum + part_sum * factor
        joint_out = joint_out + part_out * factor
    return joint_max, joint_sum, joint_out


def decode_kernel(sums_ref, cache_ref, cos_ref, sin_ref, out_ref, new_ref):
    peers = sums_ref.shape[0]
    half = (cache_ref.shape[1] - 2 * PROWS) // 2
    piece = sums_ref.shape[1] - 2 * PROWS
    total = add_projections(sums_ref)
    rotated = total * cos_ref[...] + pltpu.roll(total, HS // 2, 1) * sin_ref[...]
    query = rotated[0:QROWS].astype(BF16)
    parts = []
    for c in range(cache_ref.shape[0]):
        keys = cache_ref[c, 2 * PROWS : 2 * PROWS + half]
        values = cache_ref[c, 2 * PROWS + half : 2 * PROWS + 2 * half]
        scores = dot_t(query, keys) * SCALE
        part_max = jnp.max(scores, axis=1, keepdims=True)
        weights = jnp.exp(scores - part_max)
        part_sum = jnp.sum(weights, axis=1, keepdims=True)
        parts.append((part_max, part_sum, dot(weights.astype(BF16), values)))
    joint_max, joint_sum, joint_out = join(parts)
    stats = pack_stats(joint_max, joint_sum)
    joint_out = joint_out.astype(BF16)
    anchor = sums_ref[0, 2 * PROWS : 2 * PROWS + piece]
    for peer in range(peers):
        out_ref[peer, 0:QROWS] = joint_out
        out_ref[peer, QROWS : QROWS + SROWS] = stats
        out_ref[peer, QROWS + SROWS : QROWS + SROWS + piece] = anchor
    key_new = rotated[QROWS:PROWS].astype(BF16)
    value_new = pltpu.roll(total[QROWS:PROWS], STEPS, 0).astype(BF16)
    scores = dot_t(query, key_new) * SCALE
    step = lax.broadcasted_iota(jnp.int32, scores.shape, 0) % STEPS
    later = lax.broadcasted_iota(jnp.int32, scores.shape, 1)
    scores = jnp.where(later <= step, scores, -jnp.inf)
    new_max = jnp.max(scores, axis=1, keepdims=True)
    weights = jnp.exp(scores - new_max)
    new_sum = jnp.sum(weights, axis=1, keepdims=True)
    new_ref[0] = jnp.broadcast_to(new_max, (QROWS, HS))
    new_ref[1] = jnp.broadcast_to(new_sum, (QROWS, HS))
    new_ref[2] = dot(weights.astype(BF16), value_new)


def combine_kernel(parts_ref, new_ref, out_ref):
    peers = parts_ref.shape[0]
    first = QROWS + SROWS
    piece = parts_ref.shape[1] - first
    parts = []
    for peer in range(peers):
        part_max, part_sum = unpack_stats(parts_ref[peer, QROWS:first])
        parts.append((part_max, part_sum, parts_ref[peer, 0:QROWS].astype(F32)))
    has_new = lax.axis_index("zo") == 0
    new_max = new_ref[0][:, 0:1]
    parts.append(
        (
            jnp.where(has_new, new_max, parts[0][0]),
            jnp.where(has_new, new_ref[1][:, 0:1], 0.0),
            jnp.where(has_new, new_ref[2], 0.0),
        )
    )
    joint_max, joint_sum, joint_out = join(parts)
    high, low = split2(joint_out)
    stats = pack_stats(joint_max, joint_sum)
    for near in range(out_ref.shape[0]):
        out_ref[near, 0:QROWS] = high
        out_ref[near, QROWS : 2 * QROWS] = low
        out_ref[near, 2 * QROWS : HROWS] = stats
        for peer in range(peers):
            start = HROWS + peer * piece
            out_ref[near, start : start + piece] = parts_ref[peer, first : first + piece]


def prefill_kernel(query_ref, key_ref, value_ref, anchor_ref, out_ref, decoded_ref):
    block = key_ref.shape[0]
    half = block // 2
    group = pl.program_id(0)
    parities = anchor_ref.shape[0] // HK
    piece = (anchor_ref.shape[1] - HROWS) // 2
    use_anchor = (lax.axis_index("x") + lax.axis_index("zz") + lax.axis_index("zo")) != 0
    head_cols = pl.ds(pl.multiple_of(group * HS, HS), HS)
    key = key_ref[:, head_cols]
    near = [group * parities + parity for parity in range(parities)]
    anchor_key = jnp.concatenate([anchor_ref[n, HROWS : HROWS + piece] for n in near], axis=0)
    anchor_value = jnp.concatenate([anchor_ref[n, HROWS + piece :] for n in near], axis=0)
    parts = []
    for n in near:
        part_max, part_sum = unpack_stats(anchor_ref[n, 2 * QROWS : HROWS])
        part_out = anchor_ref[n, 0:QROWS].astype(F32) + anchor_ref[n, QROWS : 2 * QROWS].astype(F32)
        parts.append((part_max, part_sum, part_out))
    _, decoded_sum, decoded_out = join(parts)
    decoded = (decoded_out / decoded_sum).astype(BF16)
    values = jnp.concatenate([anchor_value.T, value_ref[:, head_cols].T], axis=1)
    causal = lax.broadcasted_iota(jnp.int32, (half, half), 0) <= lax.broadcasted_iota(
        jnp.int32, (half, half), 1
    )
    for j in range(GROUP):
        cols = slice(j * HS, (j + 1) * HS)
        query = query_ref[:, pl.ds(pl.multiple_of((group * GROUP + j) * HS, HS), HS)]
        anchor_scores = dot_t(anchor_key, query)
        early_scores = dot_t(key[:half], query)
        late_scores = dot_t(key[half:], query[half:])
        for part in range(2):
            rows = slice(part * half, (part + 1) * half)
            anchor = anchor_scores[:, rows]
            if part == 0:
                own = jnp.where(causal, early_scores[:, rows], -jnp.inf)
            else:
                own = jnp.concatenate(
                    [early_scores[:, rows], jnp.where(causal, late_scores, -jnp.inf)], axis=0
                )
            own_max = jnp.max(own, axis=0, keepdims=True)
            anchor_max = jnp.max(anchor, axis=0, keepdims=True)
            row_max = jnp.where(use_anchor, jnp.maximum(own_max, anchor_max), own_max)
            anchor_shift = jnp.where(use_anchor, row_max, jnp.inf)
            own_weights = jnp.exp2((own - row_max) * EXP2_SCALE)
            anchor_weights = jnp.exp2((anchor - anchor_shift) * EXP2_SCALE)
            row_sum = jnp.sum(own_weights, axis=0, keepdims=True) + jnp.sum(
                anchor_weights, axis=0, keepdims=True
            )
            weights = jnp.concatenate(
                [anchor_weights.astype(BF16), own_weights.astype(BF16)], axis=0
            )
            weighted = dot(values[:, : block + (part + 1) * half], weights)
            out_ref[rows, cols] = (weighted * (1.0 / row_sum)).T.astype(BF16)
        pick = (
            lax.broadcasted_iota(jnp.int32, (STEPS, QROWS), 1)
            == lax.broadcasted_iota(jnp.int32, (STEPS, QROWS), 0) + j * STEPS
        )
        decoded_ref[:, cols] = dot(pick.astype(BF16), decoded).astype(BF16)


def rotary_tables(position):
    shape = (PROWS, HS)
    lane = lax.broadcasted_iota(jnp.int32, shape, 1)
    step = lax.broadcasted_iota(jnp.int32, shape, 0) % STEPS
    half_width = HS // 2
    frequency = jnp.exp((lane % half_width).astype(F32) * (-2.0 * math.log(500000.0) / HS))
    angles = (position + step).astype(F32) * frequency
    sine = jnp.sin(angles)
    return jnp.cos(angles), jnp.where(lane < half_width, -sine, sine)


VMEM_SPEC = pl.BlockSpec(memory_space=pltpu.VMEM)


def in_vmem(value):
    return value if INTERPRET else pltpu.with_memory_space_constraint(value, pltpu.VMEM)


def call(kernel, out_shape, **kwargs):
    if not INTERPRET:
        out_shape = jax.tree.map(lambda out: pltpu.VMEM(out.shape, out.dtype), out_shape)
    return pl.pallas_call(
        kernel,
        out_shape=out_shape,
        out_specs=jax.tree.map(lambda _: VMEM_SPEC, out_shape),
        interpret=INTERPRET,
        **kwargs,
    )


def on_device(ctx_query, ctx_key, ctx_value, step_embed, w_query, w_key, w_value):
    block = ctx_query.shape[0]
    parities, far = lax.axis_size("zo"), lax.axis_size("zz")
    near = lax.axis_size("x") * parities
    half = block // parities
    piece = 2 * half // far
    shape = jax.ShapeDtypeStruct
    cosine, sine = rotary_tables(near * far * block)

    slabs = call(
        project_kernel,
        shape((near, 2 * PROWS + 2 * half, HS), BF16),
        name="project",
        scratch_shapes=[pltpu.VMEM((HK, PROWS, HS), F32)],
    )(step_embed, w_query, w_key, w_value, ctx_key, ctx_value)
    cache = in_vmem(lax.all_to_all(slabs, ("x", "zo"), 0, 0, tiled=True))
    spread = call(
        spread_kernel,
        shape((far, 2 * PROWS + piece, HS), BF16),
        name="spread",
        in_specs=[VMEM_SPEC],
    )(cache)
    sums = in_vmem(lax.all_to_all(spread, "zz", 0, 0, tiled=True))
    parts, new = call(
        decode_kernel,
        (shape((far, QROWS + SROWS + piece, HS), BF16), shape((3, QROWS, HS), F32)),
        name="decode",
        in_specs=[VMEM_SPEC] * 4,
    )(sums, cache, in_vmem(cosine), in_vmem(sine))
    parts = in_vmem(lax.all_to_all(parts, "zz", 0, 0, tiled=True))
    heads = call(
        combine_kernel,
        shape((near, HROWS + 2 * half, HS), BF16),
        name="combine",
        in_specs=[VMEM_SPEC] * 2,
    )(parts, in_vmem(new))
    heads = in_vmem(lax.all_to_all(heads, ("x", "zo"), 0, 0, tiled=True))
    width = GROUP * HS
    context_out, decoded = pl.pallas_call(
        prefill_kernel,
        out_shape=(shape((block, HQ * HS), BF16), shape((STEPS, HQ * HS), BF16)),
        name="prefill",
        grid=(HK,),
        in_specs=[VMEM_SPEC] * 4,
        out_specs=[
            pl.BlockSpec((block, width), lambda h: (0, h)),
            pl.BlockSpec((STEPS, width), lambda h: (0, h)),
        ],
        interpret=INTERPRET,
    )(in_vmem(ctx_query), in_vmem(ctx_key), in_vmem(ctx_value), heads)
    return context_out, decoded


def solution(mesh):
    docs, contexts = mesh.shape["doc"], mesh.shape["ctx"]
    split = Mesh(mesh.devices.reshape(docs, HK, contexts // (2 * HK), 2), ("doc", "x", "zz", "zo"))
    ctx = ("x", "zz", "zo")
    rows = P(("doc",) + ctx, None)
    return jax.shard_map(
        on_device,
        mesh=split,
        in_specs=(rows, rows, rows, P("doc", ctx), P(ctx, None), P(ctx, None), P(ctx, None)),
        out_specs=(rows, P("doc", None)),
        check_vma=False,
    )
```

```python
import functools
import math

import jax
import jax.numpy as jnp
from jax import lax
from jax.experimental import pallas as pl
from jax.experimental.pallas import tpu as pltpu
from jax.sharding import Mesh
from jax.sharding import PartitionSpec as P

HS = 128
HQ = 16
HK = 4
GROUP = 4
STEPS = 4
QROWS = GROUP * STEPS
PROWS = QROWS + 2 * STEPS
SROWS = QROWS // 2
HROWS = 2 * QROWS + SROWS
SCALE = 1.0 / math.sqrt(HS)
EXP2_SCALE = SCALE * math.log2(math.e)
BF16 = jnp.bfloat16
F32 = jnp.float32
INTERPRET = False


def dot(a, b):
    return lax.dot_general(a, b, (((1,), (0,)), ((), ())), preferred_element_type=F32)


def dot_t(a, b):
    return lax.dot_general(a, b, (((1,), (1,)), ((), ())), preferred_element_type=F32)


def split2(value):
    high = value.astype(BF16)
    return high, (value - high.astype(F32)).astype(BF16)


def split3(value):
    high = value.astype(BF16)
    rest = value - high.astype(F32)
    middle = rest.astype(BF16)
    return high, middle, (rest - middle.astype(F32)).astype(BF16)


def project_kernel(embed_ref, wq_ref, wk_ref, wv_ref, key_ref, value_ref, out_ref, part_ref):
    parities = out_ref.shape[0] // HK
    half = key_ref.shape[0] // parities
    embed = embed_ref[...]
    query, key, value = dot(embed, wq_ref[...]), dot(embed, wk_ref[...]), dot(embed, wv_ref[...])
    for group in range(HK):
        cols = slice(group * HS, (group + 1) * HS)
        for j in range(GROUP):
            head = group * GROUP + j
            part_ref[group, j * STEPS : (j + 1) * STEPS] = query[:, head * HS : (head + 1) * HS]
        part_ref[group, QROWS : QROWS + STEPS] = key[:, cols]
        part_ref[group, QROWS + STEPS : PROWS] = value[:, cols]
        for parity in range(parities):
            near = group * parities + parity
            rows = slice(parity * half, (parity + 1) * half)
            out_ref[near, 2 * PROWS : 2 * PROWS + half] = key_ref[rows, cols]
            out_ref[near, 2 * PROWS + half : 2 * PROWS + 2 * half] = value_ref[rows, cols]
    for group in range(HK):
        high, low = split2(part_ref[group])
        for parity in range(parities):
            out_ref[group * parities + parity, 0:PROWS] = high
            out_ref[group * parities + parity, PROWS : 2 * PROWS] = low


def add_projections(in_ref):
    total = in_ref[0, 0:PROWS].astype(F32) + in_ref[0, PROWS : 2 * PROWS].astype(F32)
    for source in range(1, in_ref.shape[0]):
        total = total + (
            in_ref[source, 0:PROWS].astype(F32) + in_ref[source, PROWS : 2 * PROWS].astype(F32)
        )
    return total


def spread_kernel(in_ref, out_ref):
    peers = out_ref.shape[0]
    piece = out_ref.shape[1] - 2 * PROWS
    high, low = split2(add_projections(in_ref))
    for peer in range(peers):
        out_ref[peer, 0:PROWS] = high
        out_ref[peer, PROWS : 2 * PROWS] = low
        start = 2 * PROWS + peer * piece
        out_ref[peer, 2 * PROWS : 2 * PROWS + piece] = in_ref[0, start : start + piece]


def pack_stats(part_max, part_sum):
    lane = lax.broadcasted_iota(jnp.int32, (QROWS, HS), 1)
    stats = jnp.zeros((QROWS, HS), F32)
    for at, value in enumerate(split3(part_max) + split3(part_sum)):
        stats = jnp.where(lane == at, value.astype(F32), stats)
    stats = jnp.where(lane[:SROWS] < HS // 2, stats[:SROWS], pltpu.roll(stats[SROWS:], HS // 2, 1))
    return stats.astype(BF16)


def unpack_stats(stats):
    stats = stats.astype(F32)
    stats = jnp.concatenate([stats, pltpu.roll(stats, HS // 2, 1)], axis=0)
    return (
        stats[:, 0:1] + stats[:, 1:2] + stats[:, 2:3],
        stats[:, 3:4] + stats[:, 4:5] + stats[:, 5:6],
    )


def join(parts):
    joint_max = functools.reduce(jnp.maximum, [part[0] for part in parts])
    joint_sum, joint_out = 0.0, 0.0
    for part_max, part_sum, part_out in parts:
        factor = jnp.exp(part_max - joint_max)
        joint_sum = joint_sum + part_sum * factor
        joint_out = joint_out + part_out * factor
    return joint_max, joint_sum, joint_out


def decode_kernel(sums_ref, cache_ref, cos_ref, sin_ref, out_ref, new_ref):
    peers = sums_ref.shape[0]
    half = (cache_ref.shape[1] - 2 * PROWS) // 2
    piece = sums_ref.shape[1] - 2 * PROWS
    total = add_projections(sums_ref)
    rotated = total * cos_ref[...] + pltpu.roll(total, HS // 2, 1) * sin_ref[...]
    query = rotated[0:QROWS].astype(BF16)
    sources = range(cache_ref.shape[0])
    scores = jnp.concatenate(
        [dot_t(query, cache_ref[c, 2 * PROWS : 2 * PROWS + half]) for c in sources], axis=1
    )
    scores = scores * SCALE
    joint_max = jnp.max(scores, axis=1, keepdims=True)
    weights = jnp.exp(scores - joint_max)
    joint_sum = jnp.sum(weights, axis=1, keepdims=True)
    weights = weights.astype(BF16)
    joint_out = functools.reduce(
        jnp.add,
        [
            dot(weights[:, c * half : (c + 1) * half], cache_ref[c, 2 * PROWS + half :])
            for c in sources
        ],
    )
    stats = pack_stats(joint_max, joint_sum)
    joint_out = joint_out.astype(BF16)
    anchor = sums_ref[0, 2 * PROWS : 2 * PROWS + piece]
    for peer in range(peers):
        out_ref[peer, 0:QROWS] = joint_out
        out_ref[peer, QROWS : QROWS + SROWS] = stats
        out_ref[peer, QROWS + SROWS : QROWS + SROWS + piece] = anchor
    key_new = rotated[QROWS:PROWS].astype(BF16)
    value_new = pltpu.roll(total[QROWS:PROWS], STEPS, 0).astype(BF16)
    scores = dot_t(query, key_new) * SCALE
    step = lax.broadcasted_iota(jnp.int32, scores.shape, 0) % STEPS
    later = lax.broadcasted_iota(jnp.int32, scores.shape, 1)
    scores = jnp.where(later <= step, scores, -jnp.inf)
    new_max = jnp.max(scores, axis=1, keepdims=True)
    weights = jnp.exp(scores - new_max)
    new_sum = jnp.sum(weights, axis=1, keepdims=True)
    new_ref[0] = jnp.broadcast_to(new_max, (QROWS, HS))
    new_ref[1] = jnp.broadcast_to(new_sum, (QROWS, HS))
    new_ref[2] = dot(weights.astype(BF16), value_new)


def combine_kernel(parts_ref, new_ref, out_ref):
    peers = parts_ref.shape[0]
    first = QROWS + SROWS
    piece = parts_ref.shape[1] - first
    parts = []
    for peer in range(peers):
        part_max, part_sum = unpack_stats(parts_ref[peer, QROWS:first])
        parts.append((part_max, part_sum, parts_ref[peer, 0:QROWS].astype(F32)))
    has_new = lax.axis_index("zo") == 0
    new_max = new_ref[0][:, 0:1]
    parts.append(
        (
            jnp.where(has_new, new_max, parts[0][0]),
            jnp.where(has_new, new_ref[1][:, 0:1], 0.0),
            jnp.where(has_new, new_ref[2], 0.0),
        )
    )
    joint_max, joint_sum, joint_out = join(parts)
    high, low = split2(joint_out)
    stats = pack_stats(joint_max, joint_sum)
    for near in range(out_ref.shape[0]):
        out_ref[near, 0:QROWS] = high
        out_ref[near, QROWS : 2 * QROWS] = low
        out_ref[near, 2 * QROWS : HROWS] = stats
        for peer in range(peers):
            start = HROWS + peer * piece
            out_ref[near, start : start + piece] = parts_ref[peer, first : first + piece]


def own_kernel(query_ref, key_ref, value_ref, out_ref, stats_ref):
    half = key_ref.shape[0] // 2
    key = key_ref[...]
    values = value_ref[...].T
    causal = lax.broadcasted_iota(jnp.int32, (half, half), 0) <= lax.broadcasted_iota(
        jnp.int32, (half, half), 1
    )
    for j in range(GROUP):
        query = query_ref[:, j * HS : (j + 1) * HS]
        early = dot_t(key[:half], query)
        late = dot_t(key[half:], query[half:])
        for part in range(2):
            rows = slice(part * half, (part + 1) * half)
            if part == 0:
                scores = jnp.where(causal, early[:, rows], -jnp.inf)
            else:
                late = jnp.where(causal, late, -jnp.inf)
                scores = jnp.concatenate([early[:, rows], late], axis=0)
            own_max = jnp.max(scores, axis=0, keepdims=True)
            weights = jnp.exp2((scores - own_max) * EXP2_SCALE)
            stats_ref[j, 0:1, rows] = own_max
            stats_ref[j, 1:2, rows] = jnp.sum(weights, axis=0, keepdims=True)
            out_ref[j, :, rows] = dot(values[:, : (part + 1) * half], weights.astype(BF16))


def prefill_kernel(query_ref, own_ref, own_stats_ref, anchor_ref, out_ref, decoded_ref):
    group = pl.program_id(0)
    parities = anchor_ref.shape[0] // HK
    piece = (anchor_ref.shape[1] - HROWS) // 2
    use_anchor = (lax.axis_index("x") + lax.axis_index("zz") + lax.axis_index("zo")) != 0
    near = [group * parities + parity for parity in range(parities)]
    keys = jnp.concatenate([anchor_ref[n, HROWS : HROWS + piece] for n in near], axis=0)
    values = jnp.concatenate([anchor_ref[n, HROWS + piece :] for n in near], axis=0).T

    half = out_ref.shape[0] // 2
    units = [(j, slice(part * half, (part + 1) * half)) for j in range(GROUP) for part in range(2)]

    def scores_of(j, rows):
        return dot_t(keys, query_ref[rows, j * HS : (j + 1) * HS])

    def weigh(scores, j, rows):
        own_max, own_sum = own_stats_ref[j, 0:1, rows], own_stats_ref[j, 1:2, rows]
        anchor_max = jnp.max(scores, axis=0, keepdims=True)
        row_max = jnp.where(use_anchor, jnp.maximum(own_max, anchor_max), own_max)
        shift = jnp.where(use_anchor, row_max, jnp.inf)
        weights = jnp.exp2((scores - shift) * EXP2_SCALE)
        own_factor = jnp.exp2((own_max - row_max) * EXP2_SCALE)
        row_sum = own_sum * own_factor + jnp.sum(weights, axis=0, keepdims=True)
        return weights.astype(BF16), own_factor, 1.0 / row_sum

    def finish(weighed, j, rows):
        weights, own_factor, inverse = weighed
        weighted = own_ref[j, :, rows] * own_factor + dot(values, weights)
        out_ref[rows, j * HS : (j + 1) * HS] = (weighted * inverse).T.astype(BF16)

    scores, weighed = scores_of(*units[0]), None
    for at, unit in enumerate(units):
        later = scores_of(*units[at + 1]) if at + 1 < len(units) else None
        weighing = weigh(scores, *unit)
        if weighed is not None:
            finish(weighed, *units[at - 1])
        scores, weighed = later, weighing
    finish(weighed, *units[-1])
    parts = []
    for n in near:
        part_max, part_sum = unpack_stats(anchor_ref[n, 2 * QROWS : HROWS])
        part_out = anchor_ref[n, 0:QROWS].astype(F32) + anchor_ref[n, QROWS : 2 * QROWS].astype(F32)
        parts.append((part_max, part_sum, part_out))
    _, decoded_sum, decoded_out = join(parts)
    decoded = (decoded_out / decoded_sum).astype(BF16)
    for j in range(GROUP):
        pick = (
            lax.broadcasted_iota(jnp.int32, (STEPS, QROWS), 1)
            == lax.broadcasted_iota(jnp.int32, (STEPS, QROWS), 0) + j * STEPS
        )
        decoded_ref[:, j * HS : (j + 1) * HS] = dot(pick.astype(BF16), decoded).astype(BF16)


def rotary_tables(position):
    shape = (PROWS, HS)
    lane = lax.broadcasted_iota(jnp.int32, shape, 1)
    step = lax.broadcasted_iota(jnp.int32, shape, 0) % STEPS
    half_width = HS // 2
    frequency = jnp.exp((lane % half_width).astype(F32) * (-2.0 * math.log(500000.0) / HS))
    angles = (position + step).astype(F32) * frequency
    sine = jnp.sin(angles)
    return jnp.cos(angles), jnp.where(lane < half_width, -sine, sine)


VMEM_SPEC = pl.BlockSpec(memory_space=pltpu.VMEM)


def in_vmem(value):
    return value if INTERPRET else pltpu.with_memory_space_constraint(value, pltpu.VMEM)


def call(kernel, out_shape, **kwargs):
    if not INTERPRET:
        out_shape = jax.tree.map(lambda out: pltpu.VMEM(out.shape, out.dtype), out_shape)
    return pl.pallas_call(
        kernel,
        out_shape=out_shape,
        out_specs=jax.tree.map(lambda _: VMEM_SPEC, out_shape),
        interpret=INTERPRET,
        **kwargs,
    )


def on_device(ctx_query, ctx_key, ctx_value, step_embed, w_query, w_key, w_value):
    block = ctx_query.shape[0]
    parities, far = lax.axis_size("zo"), lax.axis_size("zz")
    near = lax.axis_size("x") * parities
    half = block // parities
    piece = 2 * half // far
    shape = jax.ShapeDtypeStruct
    cosine, sine = rotary_tables(near * far * block)

    slabs = call(
        project_kernel,
        shape((near, 2 * PROWS + 2 * half, HS), BF16),
        name="project",
        scratch_shapes=[pltpu.VMEM((HK, PROWS, HS), F32)],
    )(step_embed, w_query, w_key, w_value, ctx_key, ctx_value)
    cache = in_vmem(lax.all_to_all(slabs, ("x", "zo"), 0, 0, tiled=True))
    spread = call(
        spread_kernel,
        shape((far, 2 * PROWS + piece, HS), BF16),
        name="spread",
        in_specs=[VMEM_SPEC],
    )(cache)
    sums = in_vmem(lax.all_to_all(spread, "zz", 0, 0, tiled=True))
    width = GROUP * HS
    group_cols = pl.BlockSpec((block, width), lambda h: (0, h))
    head_cols = pl.BlockSpec((block, HS), lambda h: (0, h))
    group_heads = pl.BlockSpec((GROUP, HS, block), lambda h: (h, 0, 0))
    group_stats = pl.BlockSpec((GROUP, 2, block), lambda h: (h, 0, 0))
    with jax.named_scope("own"):
        own, own_stats = pl.pallas_call(
            own_kernel,
            out_shape=(shape((HQ, HS, block), F32), shape((HQ, 2, block), F32)),
            name="own",
            grid=(HK,),
            in_specs=[group_cols, head_cols, head_cols],
            out_specs=[group_heads, group_stats],
            interpret=INTERPRET,
        )(ctx_query, ctx_key, ctx_value)
    parts, new = call(
        decode_kernel,
        (shape((far, QROWS + SROWS + piece, HS), BF16), shape((3, QROWS, HS), F32)),
        name="decode",
        in_specs=[VMEM_SPEC] * 4,
    )(sums, cache, in_vmem(cosine), in_vmem(sine))
    parts = in_vmem(lax.all_to_all(parts, "zz", 0, 0, tiled=True))
    heads = call(
        combine_kernel,
        shape((near, HROWS + 2 * half, HS), BF16),
        name="combine",
        in_specs=[VMEM_SPEC] * 2,
    )(parts, in_vmem(new))
    heads = in_vmem(lax.all_to_all(heads, ("x", "zo"), 0, 0, tiled=True))
    context_out, decoded = pl.pallas_call(
        prefill_kernel,
        out_shape=(shape((block, HQ * HS), BF16), shape((STEPS, HQ * HS), BF16)),
        name="prefill",
        grid=(HK,),
        in_specs=[group_cols, group_heads, group_stats, VMEM_SPEC],
        out_specs=[
            group_cols,
            pl.BlockSpec((STEPS, width), lambda h: (0, h)),
        ],
        interpret=INTERPRET,
    )(ctx_query, own, own_stats, heads)
    return context_out, decoded


def solution(mesh):
    docs, contexts = mesh.shape["doc"], mesh.shape["ctx"]
    split = Mesh(mesh.devices.reshape(docs, HK, contexts // (2 * HK), 2), ("doc", "x", "zz", "zo"))
    ctx = ("x", "zz", "zo")
    rows = P(("doc",) + ctx, None)
    return jax.shard_map(
        on_device,
        mesh=split,
        in_specs=(rows, rows, rows, P("doc", ctx), P(ctx, None), P(ctx, None), P(ctx, None)),
        out_specs=(rows, P("doc", None)),
        check_vma=False,
    )
```

```python
import functools
import math

import jax
import jax.numpy as jnp
from jax import lax
from jax.experimental import pallas as pl
from jax.experimental.pallas import tpu as pltpu
from jax.sharding import Mesh
from jax.sharding import PartitionSpec as P


HS = 128
HQ = 16
HK = 4
GROUP = 4
STEPS = 4
QROWS = GROUP * STEPS
PROWS = QROWS + 2 * STEPS
SROWS = QROWS // 2
HROWS = 2 * QROWS + SROWS
SCALE = 1.0 / math.sqrt(HS)
EXP2_SCALE = SCALE * math.log2(math.e)
BF16 = jnp.bfloat16
F32 = jnp.float32
INTERPRET = False


def dot(a, b):
    return lax.dot_general(a, b, (((1,), (0,)), ((), ())), preferred_element_type=F32)


def dot_t(a, b):
    return lax.dot_general(a, b, (((1,), (1,)), ((), ())), preferred_element_type=F32)


def split2(value):
    high = value.astype(BF16)
    return high, (value - high.astype(F32)).astype(BF16)


def split3(value):
    high = value.astype(BF16)
    rest = value - high.astype(F32)
    middle = rest.astype(BF16)
    return high, middle, (rest - middle.astype(F32)).astype(BF16)


def project_kernel(embed_ref, wq_ref, wk_ref, wv_ref, key_ref, value_ref, out_ref, part_ref):
    parities = out_ref.shape[0] // HK
    half = key_ref.shape[0] // parities
    embed = embed_ref[...]
    query, key, value = dot(embed, wq_ref[...]), dot(embed, wk_ref[...]), dot(embed, wv_ref[...])
    for group in range(HK):
        cols = slice(group * HS, (group + 1) * HS)
        for j in range(GROUP):
            head = group * GROUP + j
            part_ref[group, j * STEPS : (j + 1) * STEPS] = query[:, head * HS : (head + 1) * HS]
        part_ref[group, QROWS : QROWS + STEPS] = key[:, cols]
        part_ref[group, QROWS + STEPS : PROWS] = value[:, cols]
        for parity in range(parities):
            near = group * parities + parity
            rows = slice(parity * half, (parity + 1) * half)
            out_ref[near, 2 * PROWS : 2 * PROWS + half] = key_ref[rows, cols]
            out_ref[near, 2 * PROWS + half : 2 * PROWS + 2 * half] = value_ref[rows, cols]
    for group in range(HK):
        high, low = split2(part_ref[group])
        for parity in range(parities):
            out_ref[group * parities + parity, 0:PROWS] = high
            out_ref[group * parities + parity, PROWS : 2 * PROWS] = low


def add_projections(in_ref):
    total = in_ref[0, 0:PROWS].astype(F32) + in_ref[0, PROWS : 2 * PROWS].astype(F32)
    for source in range(1, in_ref.shape[0]):
        total = total + (
            in_ref[source, 0:PROWS].astype(F32) + in_ref[source, PROWS : 2 * PROWS].astype(F32)
        )
    return total


def spread_kernel(in_ref, out_ref):
    peers = out_ref.shape[0]
    piece = out_ref.shape[1] - 2 * PROWS
    high, low = split2(add_projections(in_ref))
    for peer in range(peers):
        out_ref[peer, 0:PROWS] = high
        out_ref[peer, PROWS : 2 * PROWS] = low
        start = 2 * PROWS + peer * piece
        out_ref[peer, 2 * PROWS : 2 * PROWS + piece] = in_ref[0, start : start + piece]


def pack_stats(part_max, part_sum):
    lane = lax.broadcasted_iota(jnp.int32, (QROWS, HS), 1)
    stats = jnp.zeros((QROWS, HS), F32)
    for at, value in enumerate(split3(part_max) + split3(part_sum)):
        stats = jnp.where(lane == at, value.astype(F32), stats)
    stats = jnp.where(lane[:SROWS] < HS // 2, stats[:SROWS], pltpu.roll(stats[SROWS:], HS // 2, 1))
    return stats.astype(BF16)


def unpack_stats(stats):
    stats = stats.astype(F32)
    stats = jnp.concatenate([stats, pltpu.roll(stats, HS // 2, 1)], axis=0)
    return (
        stats[:, 0:1] + stats[:, 1:2] + stats[:, 2:3],
        stats[:, 3:4] + stats[:, 4:5] + stats[:, 5:6],
    )


def join(parts):
    joint_max = functools.reduce(jnp.maximum, [part[0] for part in parts])
    joint_sum, joint_out = 0.0, 0.0
    for part_max, part_sum, part_out in parts:
        factor = jnp.exp(part_max - joint_max)
        joint_sum = joint_sum + part_sum * factor
        joint_out = joint_out + part_out * factor
    return joint_max, joint_sum, joint_out


def decode_kernel(sums_ref, cache_ref, cos_ref, sin_ref, out_ref, new_ref):
    peers = sums_ref.shape[0]
    half = (cache_ref.shape[1] - 2 * PROWS) // 2
    piece = sums_ref.shape[1] - 2 * PROWS
    total = add_projections(sums_ref)
    rotated = total * cos_ref[...] + pltpu.roll(total, HS // 2, 1) * sin_ref[...]
    query = rotated[0:QROWS].astype(BF16)
    sources = range(cache_ref.shape[0])
    scores = jnp.concatenate(
        [dot_t(query, cache_ref[c, 2 * PROWS : 2 * PROWS + half]) for c in sources], axis=1
    )
    scores = scores * SCALE
    joint_max = jnp.max(scores, axis=1, keepdims=True)
    weights = jnp.exp(scores - joint_max)
    joint_sum = jnp.sum(weights, axis=1, keepdims=True)
    weights = weights.astype(BF16)
    joint_out = functools.reduce(
        jnp.add,
        [
            dot(weights[:, c * half : (c + 1) * half], cache_ref[c, 2 * PROWS + half :])
            for c in sources
        ],
    )
    stats = pack_stats(joint_max, joint_sum)
    joint_out = joint_out.astype(BF16)
    anchor = sums_ref[0, 2 * PROWS : 2 * PROWS + piece]
    for peer in range(peers):
        out_ref[peer, 0:QROWS] = joint_out
        out_ref[peer, QROWS : QROWS + SROWS] = stats
        out_ref[peer, QROWS + SROWS : QROWS + SROWS + piece] = anchor
    key_new = rotated[QROWS:PROWS].astype(BF16)
    value_new = pltpu.roll(total[QROWS:PROWS], STEPS, 0).astype(BF16)
    scores = dot_t(query, key_new) * SCALE
    step = lax.broadcasted_iota(jnp.int32, scores.shape, 0) % STEPS
    later = lax.broadcasted_iota(jnp.int32, scores.shape, 1)
    scores = jnp.where(later <= step, scores, -jnp.inf)
    new_max = jnp.max(scores, axis=1, keepdims=True)
    weights = jnp.exp(scores - new_max)
    new_sum = jnp.sum(weights, axis=1, keepdims=True)
    new_ref[0] = jnp.broadcast_to(new_max, (QROWS, HS))
    new_ref[1] = jnp.broadcast_to(new_sum, (QROWS, HS))
    new_ref[2] = dot(weights.astype(BF16), value_new)


def combine_kernel(parts_ref, new_ref, out_ref):
    peers = parts_ref.shape[0]
    first = QROWS + SROWS
    piece = parts_ref.shape[1] - first
    parts = []
    for peer in range(peers):
        part_max, part_sum = unpack_stats(parts_ref[peer, QROWS:first])
        parts.append((part_max, part_sum, parts_ref[peer, 0:QROWS].astype(F32)))
    has_new = lax.axis_index("zo") == 0
    new_max = new_ref[0][:, 0:1]
    parts.append(
        (
            jnp.where(has_new, new_max, parts[0][0]),
            jnp.where(has_new, new_ref[1][:, 0:1], 0.0),
            jnp.where(has_new, new_ref[2], 0.0),
        )
    )
    joint_max, joint_sum, joint_out = join(parts)
    high, low = split2(joint_out)
    stats = pack_stats(joint_max, joint_sum)
    for near in range(out_ref.shape[0]):
        out_ref[near, 0:QROWS] = high
        out_ref[near, QROWS : 2 * QROWS] = low
        out_ref[near, 2 * QROWS : HROWS] = stats
        for peer in range(peers):
            start = HROWS + peer * piece
            out_ref[near, start : start + piece] = parts_ref[peer, first : first + piece]


def own_kernel(query_ref, key_ref, value_ref, out_ref, stats_ref):
    half = key_ref.shape[0] // 2
    key = key_ref[...]
    values = value_ref[...].T
    causal = lax.broadcasted_iota(jnp.int32, (half, half), 0) <= lax.broadcasted_iota(
        jnp.int32, (half, half), 1
    )
    for j in range(GROUP):
        head = pl.program_id(0) * GROUP + j
        query = query_ref[:, j * HS : (j + 1) * HS]
        early = dot_t(key[:half], query)
        late = dot_t(key[half:], query[half:])
        for part in range(2):
            rows = slice(part * half, (part + 1) * half)
            if part == 0:
                scores = jnp.where(causal, early[:, rows], -jnp.inf)
            else:
                late = jnp.where(causal, late, -jnp.inf)
                scores = jnp.concatenate([early[:, rows], late], axis=0)
            own_max = jnp.max(scores, axis=0, keepdims=True)
            weights = jnp.exp2((scores - own_max) * EXP2_SCALE)
            stats_ref[head, 0:1, rows] = own_max
            stats_ref[head, 1:2, rows] = jnp.sum(weights, axis=0, keepdims=True)
            weighted = dot(values[:, : (part + 1) * half], weights.astype(BF16))
            out_ref[head, :, rows] = weighted.astype(BF16)


def prefill_kernel(query_ref, own_ref, own_stats_ref, anchor_ref, out_ref, decoded_ref):
    group = pl.program_id(0)
    parities = anchor_ref.shape[0] // HK
    piece = (anchor_ref.shape[1] - HROWS) // 2
    use_anchor = (lax.axis_index("x") + lax.axis_index("zz") + lax.axis_index("zo")) != 0
    near = [group * parities + parity for parity in range(parities)]
    keys = jnp.concatenate([anchor_ref[n, HROWS : HROWS + piece] for n in near], axis=0)
    values = jnp.concatenate([anchor_ref[n, HROWS + piece :] for n in near], axis=0).T

    half = out_ref.shape[0] // 2
    units = [(j, slice(part * half, (part + 1) * half)) for j in range(GROUP) for part in range(2)]

    def scores_of(j, rows):
        return dot_t(keys, query_ref[rows, j * HS : (j + 1) * HS])

    def weigh(scores, j, rows):
        head = group * GROUP + j
        own_max, own_sum = own_stats_ref[head, 0:1, rows], own_stats_ref[head, 1:2, rows]
        anchor_max = jnp.max(scores, axis=0, keepdims=True)
        row_max = jnp.where(use_anchor, jnp.maximum(own_max, anchor_max), own_max)
        shift = jnp.where(use_anchor, row_max, jnp.inf)
        weights = jnp.exp2((scores - shift) * EXP2_SCALE)
        own_factor = jnp.exp2((own_max - row_max) * EXP2_SCALE)
        row_sum = own_sum * own_factor + jnp.sum(weights, axis=0, keepdims=True)
        return weights.astype(BF16), own_factor, 1.0 / row_sum

    def finish(weighed, j, rows):
        weights, own_factor, inverse = weighed
        own = own_ref[group * GROUP + j, :, rows].astype(F32)
        weighted = own * own_factor + dot(values, weights)
        out_ref[rows, j * HS : (j + 1) * HS] = (weighted * inverse).T.astype(BF16)

    scores, weighed = scores_of(*units[0]), None
    for at, unit in enumerate(units):
        later = scores_of(*units[at + 1]) if at + 1 < len(units) else None
        weighing = weigh(scores, *unit)
        if weighed is not None:
            finish(weighed, *units[at - 1])
        scores, weighed = later, weighing
    finish(weighed, *units[-1])
    parts = []
    for n in near:
        part_max, part_sum = unpack_stats(anchor_ref[n, 2 * QROWS : HROWS])
        part_out = anchor_ref[n, 0:QROWS].astype(F32) + anchor_ref[n, QROWS : 2 * QROWS].astype(F32)
        parts.append((part_max, part_sum, part_out))
    _, decoded_sum, decoded_out = join(parts)
    decoded = (decoded_out / decoded_sum).astype(BF16)
    for j in range(GROUP):
        pick = (
            lax.broadcasted_iota(jnp.int32, (STEPS, QROWS), 1)
            == lax.broadcasted_iota(jnp.int32, (STEPS, QROWS), 0) + j * STEPS
        )
        decoded_ref[:, j * HS : (j + 1) * HS] = dot(pick.astype(BF16), decoded).astype(BF16)


def rotary_tables(position):
    shape = (PROWS, HS)
    lane = lax.broadcasted_iota(jnp.int32, shape, 1)
    step = lax.broadcasted_iota(jnp.int32, shape, 0) % STEPS
    half_width = HS // 2
    frequency = jnp.exp((lane % half_width).astype(F32) * (-2.0 * math.log(500000.0) / HS))
    angles = (position + step).astype(F32) * frequency
    sine = jnp.sin(angles)
    return jnp.cos(angles), jnp.where(lane < half_width, -sine, sine)


VMEM_SPEC = pl.BlockSpec(memory_space=pltpu.VMEM)


def in_vmem(value):
    return value if INTERPRET else pltpu.with_memory_space_constraint(value, pltpu.VMEM)


def call(kernel, out_shape, **kwargs):
    if not INTERPRET:
        out_shape = jax.tree.map(lambda out: pltpu.VMEM(out.shape, out.dtype), out_shape)
    return pl.pallas_call(
        kernel,
        out_shape=out_shape,
        out_specs=jax.tree.map(lambda _: VMEM_SPEC, out_shape),
        interpret=INTERPRET,
        **kwargs,
    )


def layer(ctx_query, ctx_key, ctx_value, step_embed, w_query, w_key, w_value):
    block = ctx_query.shape[0]
    parities, far = lax.axis_size("zo"), lax.axis_size("zz")
    near = lax.axis_size("x") * parities
    half = block // parities
    piece = 2 * half // far
    shape = jax.ShapeDtypeStruct
    cosine, sine = rotary_tables(near * far * block)

    slabs = call(
        project_kernel,
        shape((near, 2 * PROWS + 2 * half, HS), BF16),
        name="project",
        scratch_shapes=[pltpu.VMEM((HK, PROWS, HS), F32)],
    )(step_embed, w_query, w_key, w_value, ctx_key, ctx_value)
    cache = in_vmem(lax.all_to_all(slabs, ("x", "zo"), 0, 0, tiled=True))
    spread = call(
        spread_kernel,
        shape((far, 2 * PROWS + piece, HS), BF16),
        name="spread",
        in_specs=[VMEM_SPEC],
    )(cache)
    sums = lax.all_to_all(spread, "zz", 0, 0, tiled=True)
    sums = in_vmem(sums)
    width = GROUP * HS
    group_cols = pl.BlockSpec((block, width), lambda h: (0, h))
    head_cols = pl.BlockSpec((block, HS), lambda h: (0, h))
    own, own_stats = call(
        own_kernel,
        (shape((HQ, HS, block), BF16), shape((HQ, 2, block), F32)),
        name="own",
        grid=(HK,),
        in_specs=[group_cols, head_cols, head_cols],
    )(ctx_query, ctx_key, ctx_value)
    parts, new = call(
        decode_kernel,
        (shape((far, QROWS + SROWS + piece, HS), BF16), shape((3, QROWS, HS), F32)),
        name="decode",
        in_specs=[VMEM_SPEC] * 4,
    )(sums, cache, in_vmem(cosine), in_vmem(sine))
    parts = in_vmem(lax.all_to_all(parts, "zz", 0, 0, tiled=True))
    heads = call(
        combine_kernel,
        shape((near, HROWS + 2 * half, HS), BF16),
        name="combine",
        in_specs=[VMEM_SPEC] * 2,
    )(parts, in_vmem(new))
    heads = in_vmem(lax.all_to_all(heads, ("x", "zo"), 0, 0, tiled=True))
    context_out, decoded = pl.pallas_call(
        prefill_kernel,
        out_shape=(shape((block, HQ * HS), BF16), shape((STEPS, HQ * HS), BF16)),
        name="prefill",
        grid=(HK,),
        in_specs=[group_cols] + [VMEM_SPEC] * 3,
        out_specs=[
            group_cols,
            pl.BlockSpec((STEPS, width), lambda h: (0, h)),
        ],
        interpret=INTERPRET,
    )(ctx_query, in_vmem(own), in_vmem(own_stats), heads)
    return context_out, decoded


def solution(mesh):
    docs, contexts = mesh.shape["doc"], mesh.shape["ctx"]
    split = Mesh(mesh.devices.reshape(docs, HK, contexts // (2 * HK), 2), ("doc", "x", "zz", "zo"))
    ctx = ("x", "zz", "zo")
    rows = P(("doc",) + ctx, None)
    return jax.shard_map(
        layer,
        mesh=split,
        in_specs=(rows, rows, rows, P("doc", ctx), P(ctx, None), P(ctx, None), P(ctx, None)),
        out_specs=(rows, P("doc", None)),
        check_vma=False,
    )
```

```python
import functools
import math

import jax
import jax.numpy as jnp
from jax import lax
from jax.experimental import pallas as pl
from jax.experimental.pallas import tpu as pltpu
from jax.sharding import Mesh
from jax.sharding import PartitionSpec as P


HS = 128
HQ = 16
HK = 4
GROUP = 4
STEPS = 4
QROWS = GROUP * STEPS
PROWS = QROWS + 2 * STEPS
SROWS = QROWS // 2
HROWS = 2 * QROWS + SROWS
SCALE = 1.0 / math.sqrt(HS)
EXP2_SCALE = SCALE * math.log2(math.e)
BF16 = jnp.bfloat16
F32 = jnp.float32
INTERPRET = False


def dot(a, b):
    return lax.dot_general(a, b, (((1,), (0,)), ((), ())), preferred_element_type=F32)


def dot_t(a, b):
    return lax.dot_general(a, b, (((1,), (1,)), ((), ())), preferred_element_type=F32)


def split2(value):
    high = value.astype(BF16)
    return high, (value - high.astype(F32)).astype(BF16)


def split3(value):
    high = value.astype(BF16)
    rest = value - high.astype(F32)
    middle = rest.astype(BF16)
    return high, middle, (rest - middle.astype(F32)).astype(BF16)


def project_kernel(embed_ref, wq_ref, wk_ref, wv_ref, key_ref, value_ref, out_ref, part_ref):
    parities = out_ref.shape[0] // HK
    half = key_ref.shape[0] // parities
    embed = embed_ref[...]
    query, key, value = dot(embed, wq_ref[...]), dot(embed, wk_ref[...]), dot(embed, wv_ref[...])
    for group in range(HK):
        cols = slice(group * HS, (group + 1) * HS)
        for j in range(GROUP):
            head = group * GROUP + j
            part_ref[group, j * STEPS : (j + 1) * STEPS] = query[:, head * HS : (head + 1) * HS]
        part_ref[group, QROWS : QROWS + STEPS] = key[:, cols]
        part_ref[group, QROWS + STEPS : PROWS] = value[:, cols]
        for parity in range(parities):
            near = group * parities + parity
            rows = slice(parity * half, (parity + 1) * half)
            out_ref[near, 2 * PROWS : 2 * PROWS + half] = key_ref[rows, cols]
            out_ref[near, 2 * PROWS + half : 2 * PROWS + 2 * half] = value_ref[rows, cols]
    for group in range(HK):
        high, low = split2(part_ref[group])
        for parity in range(parities):
            out_ref[group * parities + parity, 0:PROWS] = high
            out_ref[group * parities + parity, PROWS : 2 * PROWS] = low


def add_projections(in_ref):
    total = in_ref[0, 0:PROWS].astype(F32) + in_ref[0, PROWS : 2 * PROWS].astype(F32)
    for source in range(1, in_ref.shape[0]):
        total = total + (
            in_ref[source, 0:PROWS].astype(F32) + in_ref[source, PROWS : 2 * PROWS].astype(F32)
        )
    return total


def spread_kernel(in_ref, out_ref):
    peers = out_ref.shape[0]
    piece = out_ref.shape[1] - 2 * PROWS
    high, low = split2(add_projections(in_ref))
    for peer in range(peers):
        out_ref[peer, 0:PROWS] = high
        out_ref[peer, PROWS : 2 * PROWS] = low
        start = 2 * PROWS + peer * piece
        out_ref[peer, 2 * PROWS : 2 * PROWS + piece] = in_ref[0, start : start + piece]


def pack_stats(part_max, part_sum):
    lane = lax.broadcasted_iota(jnp.int32, (QROWS, HS), 1)
    stats = jnp.zeros((QROWS, HS), F32)
    for at, value in enumerate(split3(part_max) + split3(part_sum)):
        stats = jnp.where(lane == at, value.astype(F32), stats)
    stats = jnp.where(lane[:SROWS] < HS // 2, stats[:SROWS], pltpu.roll(stats[SROWS:], HS // 2, 1))
    return stats.astype(BF16)


def unpack_stats(stats):
    stats = stats.astype(F32)
    stats = jnp.concatenate([stats, pltpu.roll(stats, HS // 2, 1)], axis=0)
    return (
        stats[:, 0:1] + stats[:, 1:2] + stats[:, 2:3],
        stats[:, 3:4] + stats[:, 4:5] + stats[:, 5:6],
    )


def join(parts):
    joint_max = functools.reduce(jnp.maximum, [part[0] for part in parts])
    joint_sum, joint_out = 0.0, 0.0
    for part_max, part_sum, part_out in parts:
        factor = jnp.exp(part_max - joint_max)
        joint_sum = joint_sum + part_sum * factor
        joint_out = joint_out + part_out * factor
    return joint_max, joint_sum, joint_out


def decode_kernel(sums_ref, cache_ref, cos_ref, sin_ref, out_ref, new_ref):
    peers = sums_ref.shape[0]
    half = (cache_ref.shape[1] - 2 * PROWS) // 2
    piece = sums_ref.shape[1] - 2 * PROWS
    total = add_projections(sums_ref)
    rotated = total * cos_ref[...] + pltpu.roll(total, HS // 2, 1) * sin_ref[...]
    query = rotated[0:QROWS].astype(BF16)
    sources = range(cache_ref.shape[0])
    scores = jnp.concatenate(
        [dot_t(query, cache_ref[c, 2 * PROWS : 2 * PROWS + half]) for c in sources], axis=1
    )
    scores = scores * SCALE
    joint_max = jnp.max(scores, axis=1, keepdims=True)
    weights = jnp.exp(scores - joint_max)
    joint_sum = jnp.sum(weights, axis=1, keepdims=True)
    weights = weights.astype(BF16)
    joint_out = functools.reduce(
        jnp.add,
        [
            dot(weights[:, c * half : (c + 1) * half], cache_ref[c, 2 * PROWS + half :])
            for c in sources
        ],
    )
    stats = pack_stats(joint_max, joint_sum)
    joint_out = joint_out.astype(BF16)
    anchor = sums_ref[peers // 2, 2 * PROWS : 2 * PROWS + piece]
    for peer in range(peers):
        out_ref[peer, 0:QROWS] = joint_out
        out_ref[peer, QROWS : QROWS + SROWS] = stats
        out_ref[peer, QROWS + SROWS : QROWS + SROWS + piece] = anchor
    key_new = rotated[QROWS:PROWS].astype(BF16)
    value_new = pltpu.roll(total[QROWS:PROWS], STEPS, 0).astype(BF16)
    scores = dot_t(query, key_new) * SCALE
    step = lax.broadcasted_iota(jnp.int32, scores.shape, 0) % STEPS
    later = lax.broadcasted_iota(jnp.int32, scores.shape, 1)
    scores = jnp.where(later <= step, scores, -jnp.inf)
    new_max = jnp.max(scores, axis=1, keepdims=True)
    weights = jnp.exp(scores - new_max)
    new_sum = jnp.sum(weights, axis=1, keepdims=True)
    new_ref[0] = jnp.broadcast_to(new_max, (QROWS, HS))
    new_ref[1] = jnp.broadcast_to(new_sum, (QROWS, HS))
    new_ref[2] = dot(weights.astype(BF16), value_new)


def combine_kernel(parts_ref, new_ref, out_ref):
    peers = parts_ref.shape[0]
    first = QROWS + SROWS
    piece = parts_ref.shape[1] - first
    parts = []
    for peer in range(peers):
        part_max, part_sum = unpack_stats(parts_ref[peer, QROWS:first])
        parts.append((part_max, part_sum, parts_ref[peer, 0:QROWS].astype(F32)))
    has_new = lax.axis_index("zo") == 0
    new_max = new_ref[0][:, 0:1]
    parts.append(
        (
            jnp.where(has_new, new_max, parts[0][0]),
            jnp.where(has_new, new_ref[1][:, 0:1], 0.0),
            jnp.where(has_new, new_ref[2], 0.0),
        )
    )
    joint_max, joint_sum, joint_out = join(parts)
    high, low = split2(joint_out)
    stats = pack_stats(joint_max, joint_sum)
    for near in range(out_ref.shape[0]):
        out_ref[near, 0:QROWS] = high
        out_ref[near, QROWS : 2 * QROWS] = low
        out_ref[near, 2 * QROWS : HROWS] = stats
        for peer in range(peers):
            start = HROWS + peer * piece
            out_ref[near, start : start + piece] = parts_ref[peer, first : first + piece]


def own_kernel(query_ref, key_ref, value_ref, out_ref, stats_ref):
    half = key_ref.shape[0] // 2
    key = key_ref[...]
    values = value_ref[...].T
    causal = lax.broadcasted_iota(jnp.int32, (half, half), 0) <= lax.broadcasted_iota(
        jnp.int32, (half, half), 1
    )
    for j in range(GROUP):
        head = pl.program_id(0) * GROUP + j
        query = query_ref[:, j * HS : (j + 1) * HS]
        early = dot_t(key[:half], query)
        late = dot_t(key[half:], query[half:])
        for part in range(2):
            rows = slice(part * half, (part + 1) * half)
            if part == 0:
                scores = jnp.where(causal, early[:, rows], -jnp.inf)
            else:
                late = jnp.where(causal, late, -jnp.inf)
                scores = jnp.concatenate([early[:, rows], late], axis=0)
            own_max = jnp.max(scores, axis=0, keepdims=True)
            weights = jnp.exp2((scores - own_max) * EXP2_SCALE)
            stats_ref[head, 0:1, rows] = own_max
            stats_ref[head, 1:2, rows] = jnp.sum(weights, axis=0, keepdims=True)
            weighted = dot(values[:, : (part + 1) * half], weights.astype(BF16))
            out_ref[head, :, rows] = weighted.astype(BF16)


def prefill_kernel(query_ref, own_ref, own_stats_ref, anchor_ref, out_ref, decoded_ref):
    group = pl.program_id(0)
    parities = anchor_ref.shape[0] // HK
    piece = (anchor_ref.shape[1] - HROWS) // 2
    use_anchor = (lax.axis_index("x") + lax.axis_index("zz") + lax.axis_index("zo")) != 0
    near = [group * parities + parity for parity in range(parities)]
    keys = jnp.concatenate([anchor_ref[n, HROWS : HROWS + piece] for n in near], axis=0)
    values = jnp.concatenate([anchor_ref[n, HROWS + piece :] for n in near], axis=0).T

    half = out_ref.shape[0] // 2
    units = [(j, slice(part * half, (part + 1) * half)) for j in range(GROUP) for part in range(2)]

    def scores_of(j, rows):
        return dot_t(keys, query_ref[rows, j * HS : (j + 1) * HS])

    def weigh(scores, j, rows):
        head = group * GROUP + j
        own_max, own_sum = own_stats_ref[head, 0:1, rows], own_stats_ref[head, 1:2, rows]
        anchor_max = jnp.max(scores, axis=0, keepdims=True)
        row_max = jnp.where(use_anchor, jnp.maximum(own_max, anchor_max), own_max)
        shift = jnp.where(use_anchor, row_max, jnp.inf)
        weights = jnp.exp2((scores - shift) * EXP2_SCALE)
        own_factor = jnp.exp2((own_max - row_max) * EXP2_SCALE)
        row_sum = own_sum * own_factor + jnp.sum(weights, axis=0, keepdims=True)
        return weights.astype(BF16), own_factor, 1.0 / row_sum

    def finish(weighed, j, rows):
        weights, own_factor, inverse = weighed
        own = own_ref[group * GROUP + j, :, rows].astype(F32)
        weighted = own * own_factor + dot(values, weights)
        out_ref[rows, j * HS : (j + 1) * HS] = (weighted * inverse).T.astype(BF16)

    scores, weighed = scores_of(*units[0]), None
    for at, unit in enumerate(units):
        later = scores_of(*units[at + 1]) if at + 1 < len(units) else None
        weighing = weigh(scores, *unit)
        if weighed is not None:
            finish(weighed, *units[at - 1])
        scores, weighed = later, weighing
    finish(weighed, *units[-1])
    parts = []
    for n in near:
        part_max, part_sum = unpack_stats(anchor_ref[n, 2 * QROWS : HROWS])
        part_out = anchor_ref[n, 0:QROWS].astype(F32) + anchor_ref[n, QROWS : 2 * QROWS].astype(F32)
        parts.append((part_max, part_sum, part_out))
    _, decoded_sum, decoded_out = join(parts)
    decoded = (decoded_out / decoded_sum).astype(BF16)
    for j in range(GROUP):
        pick = (
            lax.broadcasted_iota(jnp.int32, (STEPS, QROWS), 1)
            == lax.broadcasted_iota(jnp.int32, (STEPS, QROWS), 0) + j * STEPS
        )
        decoded_ref[:, j * HS : (j + 1) * HS] = dot(pick.astype(BF16), decoded).astype(BF16)


def rotary_tables(position):
    shape = (PROWS, HS)
    lane = lax.broadcasted_iota(jnp.int32, shape, 1)
    step = lax.broadcasted_iota(jnp.int32, shape, 0) % STEPS
    half_width = HS // 2
    frequency = jnp.exp((lane % half_width).astype(F32) * (-2.0 * math.log(500000.0) / HS))
    angles = (position + step).astype(F32) * frequency
    sine = jnp.sin(angles)
    return jnp.cos(angles), jnp.where(lane < half_width, -sine, sine)


VMEM_SPEC = pl.BlockSpec(memory_space=pltpu.VMEM)


def in_vmem(value):
    return value if INTERPRET else pltpu.with_memory_space_constraint(value, pltpu.VMEM)


def call(kernel, out_shape, **kwargs):
    if not INTERPRET:
        out_shape = jax.tree.map(lambda out: pltpu.VMEM(out.shape, out.dtype), out_shape)
    return pl.pallas_call(
        kernel,
        out_shape=out_shape,
        out_specs=jax.tree.map(lambda _: VMEM_SPEC, out_shape),
        interpret=INTERPRET,
        **kwargs,
    )


def exchange_far(value):
    far = lax.axis_size("zz")
    order = [(at + far // 2) % far for at in range(far)]
    return lax.all_to_all(value, "zz", 0, 0, axis_index_groups=[order], tiled=True)


def layer(ctx_query, ctx_key, ctx_value, step_embed, w_query, w_key, w_value):
    block = ctx_query.shape[0]
    parities, far = lax.axis_size("zo"), lax.axis_size("zz")
    near = lax.axis_size("x") * parities
    half = block // parities
    piece = 2 * half // far
    shape = jax.ShapeDtypeStruct
    cosine, sine = rotary_tables(near * far * block)

    slabs = call(
        project_kernel,
        shape((near, 2 * PROWS + 2 * half, HS), BF16),
        name="project",
        scratch_shapes=[pltpu.VMEM((HK, PROWS, HS), F32)],
    )(step_embed, w_query, w_key, w_value, ctx_key, ctx_value)
    cache = in_vmem(lax.all_to_all(slabs, ("x", "zo"), 0, 0, tiled=True))
    spread = call(
        spread_kernel,
        shape((far, 2 * PROWS + piece, HS), BF16),
        name="spread",
        in_specs=[VMEM_SPEC],
    )(cache)
    sums = exchange_far(spread)
    sums = in_vmem(sums)
    width = GROUP * HS
    group_cols = pl.BlockSpec((block, width), lambda h: (0, h))
    head_cols = pl.BlockSpec((block, HS), lambda h: (0, h))
    own, own_stats = call(
        own_kernel,
        (shape((HQ, HS, block), BF16), shape((HQ, 2, block), F32)),
        name="own",
        grid=(HK,),
        in_specs=[group_cols, head_cols, head_cols],
    )(ctx_query, ctx_key, ctx_value)
    parts, new = call(
        decode_kernel,
        (shape((far, QROWS + SROWS + piece, HS), BF16), shape((3, QROWS, HS), F32)),
        name="decode",
        in_specs=[VMEM_SPEC] * 4,
    )(sums, cache, in_vmem(cosine), in_vmem(sine))
    parts = in_vmem(exchange_far(parts))
    heads = call(
        combine_kernel,
        shape((near, HROWS + 2 * half, HS), BF16),
        name="combine",
        in_specs=[VMEM_SPEC] * 2,
    )(parts, in_vmem(new))
    heads = in_vmem(lax.all_to_all(heads, ("x", "zo"), 0, 0, tiled=True))
    context_out, decoded = pl.pallas_call(
        prefill_kernel,
        out_shape=(shape((block, HQ * HS), BF16), shape((STEPS, HQ * HS), BF16)),
        name="prefill",
        grid=(HK,),
        in_specs=[group_cols] + [VMEM_SPEC] * 3,
        out_specs=[
            group_cols,
            pl.BlockSpec((STEPS, width), lambda h: (0, h)),
        ],
        interpret=INTERPRET,
    )(ctx_query, in_vmem(own), in_vmem(own_stats), heads)
    return context_out, decoded


def solution(mesh):
    docs, contexts = mesh.shape["doc"], mesh.shape["ctx"]
    split = Mesh(mesh.devices.reshape(docs, HK, contexts // (2 * HK), 2), ("doc", "x", "zz", "zo"))
    ctx = ("x", "zz", "zo")
    rows = P(("doc",) + ctx, None)
    return jax.shard_map(
        layer,
        mesh=split,
        in_specs=(rows, rows, rows, P("doc", ctx), P(ctx, None), P(ctx, None), P(ctx, None)),
        out_specs=(rows, P("doc", None)),
        check_vma=False,
    )
```

```python
import functools
import math

import jax
import jax.numpy as jnp
from jax import lax
from jax.experimental import pallas as pl
from jax.experimental.pallas import tpu as pltpu
from jax.sharding import PartitionSpec as P


HS = 128
HQ = 16
HK = 4
GROUP = 4
STEPS = 4
QROWS = GROUP * STEPS
PROWS = QROWS + 2 * STEPS
SROWS = QROWS // 2
HROWS = 2 * QROWS + SROWS
SCALE = 1.0 / math.sqrt(HS)
EXP2_SCALE = SCALE * math.log2(math.e)
PARITIES = 2
NEAR = HK * PARITIES
BF16 = jnp.bfloat16
F32 = jnp.float32
INTERPRET = False


def dot(a, b):
    return lax.dot_general(a, b, (((1,), (0,)), ((), ())), preferred_element_type=F32)


def dot_t(a, b):
    return lax.dot_general(a, b, (((1,), (1,)), ((), ())), preferred_element_type=F32)


def split2(value):
    high = value.astype(BF16)
    return high, (value - high.astype(F32)).astype(BF16)


def split3(value):
    high = value.astype(BF16)
    rest = value - high.astype(F32)
    middle = rest.astype(BF16)
    return high, middle, (rest - middle.astype(F32)).astype(BF16)


def project_kernel(embed_ref, wq_ref, wk_ref, wv_ref, key_ref, value_ref, out_ref, part_ref):
    parities = out_ref.shape[0] // HK
    half = key_ref.shape[0] // parities
    embed = embed_ref[...]
    query, key, value = dot(embed, wq_ref[...]), dot(embed, wk_ref[...]), dot(embed, wv_ref[...])
    for group in range(HK):
        cols = slice(group * HS, (group + 1) * HS)
        for j in range(GROUP):
            head = group * GROUP + j
            part_ref[group, j * STEPS : (j + 1) * STEPS] = query[:, head * HS : (head + 1) * HS]
        part_ref[group, QROWS : QROWS + STEPS] = key[:, cols]
        part_ref[group, QROWS + STEPS : PROWS] = value[:, cols]
        for parity in range(parities):
            near = group * parities + parity
            rows = slice(parity * half, (parity + 1) * half)
            out_ref[near, 2 * PROWS : 2 * PROWS + half] = key_ref[rows, cols]
            out_ref[near, 2 * PROWS + half : 2 * PROWS + 2 * half] = value_ref[rows, cols]
    for group in range(HK):
        high, low = split2(part_ref[group])
        for parity in range(parities):
            out_ref[group * parities + parity, 0:PROWS] = high
            out_ref[group * parities + parity, PROWS : 2 * PROWS] = low


def add_projections(in_ref):
    total = in_ref[0, 0:PROWS].astype(F32) + in_ref[0, PROWS : 2 * PROWS].astype(F32)
    for source in range(1, in_ref.shape[0]):
        total = total + (
            in_ref[source, 0:PROWS].astype(F32) + in_ref[source, PROWS : 2 * PROWS].astype(F32)
        )
    return total


def spread_kernel(in_ref, out_ref):
    anchor = in_ref.shape[0] // 2
    peers = out_ref.shape[0]
    piece = out_ref.shape[1] - 2 * PROWS
    high, low = split2(add_projections(in_ref))
    for peer in range(peers):
        out_ref[peer, 0:PROWS] = high
        out_ref[peer, PROWS : 2 * PROWS] = low
        start = 2 * PROWS + peer * piece
        out_ref[peer, 2 * PROWS : 2 * PROWS + piece] = in_ref[anchor, start : start + piece]


def pack_stats(part_max, part_sum):
    lane = lax.broadcasted_iota(jnp.int32, (QROWS, HS), 1)
    stats = jnp.zeros((QROWS, HS), F32)
    for at, value in enumerate(split3(part_max) + split3(part_sum)):
        stats = jnp.where(lane == at, value.astype(F32), stats)
    stats = jnp.where(lane[:SROWS] < HS // 2, stats[:SROWS], pltpu.roll(stats[SROWS:], HS // 2, 1))
    return stats.astype(BF16)


def unpack_stats(stats):
    stats = stats.astype(F32)
    stats = jnp.concatenate([stats, pltpu.roll(stats, HS // 2, 1)], axis=0)
    return (
        stats[:, 0:1] + stats[:, 1:2] + stats[:, 2:3],
        stats[:, 3:4] + stats[:, 4:5] + stats[:, 5:6],
    )


def join(parts):
    joint_max = functools.reduce(jnp.maximum, [part[0] for part in parts])
    joint_sum, joint_out = 0.0, 0.0
    for part_max, part_sum, part_out in parts:
        factor = jnp.exp(part_max - joint_max)
        joint_sum = joint_sum + part_sum * factor
        joint_out = joint_out + part_out * factor
    return joint_max, joint_sum, joint_out


def decode_kernel(sums_ref, cache_ref, cos_ref, sin_ref, out_ref, new_ref):
    peers = sums_ref.shape[0]
    half = (cache_ref.shape[1] - 2 * PROWS) // 2
    piece = sums_ref.shape[1] - 2 * PROWS
    total = add_projections(sums_ref)
    rotated = total * cos_ref[...] + pltpu.roll(total, HS // 2, 1) * sin_ref[...]
    query = rotated[0:QROWS].astype(BF16)
    sources = range(cache_ref.shape[0])
    scores = jnp.concatenate(
        [dot_t(query, cache_ref[c, 2 * PROWS : 2 * PROWS + half]) for c in sources], axis=1
    )
    scores = scores * SCALE
    joint_max = jnp.max(scores, axis=1, keepdims=True)
    weights = jnp.exp(scores - joint_max)
    joint_sum = jnp.sum(weights, axis=1, keepdims=True)
    weights = weights.astype(BF16)
    joint_out = functools.reduce(
        jnp.add,
        [
            dot(weights[:, c * half : (c + 1) * half], cache_ref[c, 2 * PROWS + half :])
            for c in sources
        ],
    )
    stats = pack_stats(joint_max, joint_sum)
    joint_out = joint_out.astype(BF16)
    anchor = sums_ref[peers // 2, 2 * PROWS : 2 * PROWS + piece]
    for peer in range(peers):
        out_ref[peer, 0:QROWS] = joint_out
        out_ref[peer, QROWS : QROWS + SROWS] = stats
        out_ref[peer, QROWS + SROWS : QROWS + SROWS + piece] = anchor
    key_new = rotated[QROWS:PROWS].astype(BF16)
    value_new = pltpu.roll(total[QROWS:PROWS], STEPS, 0).astype(BF16)
    scores = dot_t(query, key_new) * SCALE
    step = lax.broadcasted_iota(jnp.int32, scores.shape, 0) % STEPS
    later = lax.broadcasted_iota(jnp.int32, scores.shape, 1)
    scores = jnp.where(later <= step, scores, -jnp.inf)
    new_max = jnp.max(scores, axis=1, keepdims=True)
    weights = jnp.exp(scores - new_max)
    new_sum = jnp.sum(weights, axis=1, keepdims=True)
    new_ref[0] = jnp.broadcast_to(new_max, (QROWS, HS))
    new_ref[1] = jnp.broadcast_to(new_sum, (QROWS, HS))
    new_ref[2] = dot(weights.astype(BF16), value_new)


def combine_kernel(parts_ref, new_ref, out_ref):
    peers = parts_ref.shape[0]
    first = QROWS + SROWS
    piece = parts_ref.shape[1] - first
    parts = []
    for peer in range(peers):
        part_max, part_sum = unpack_stats(parts_ref[peer, QROWS:first])
        parts.append((part_max, part_sum, parts_ref[peer, 0:QROWS].astype(F32)))
    has_new = lax.axis_index("ctx") % PARITIES == 0
    new_max = new_ref[0][:, 0:1]
    parts.append(
        (
            jnp.where(has_new, new_max, parts[0][0]),
            jnp.where(has_new, new_ref[1][:, 0:1], 0.0),
            jnp.where(has_new, new_ref[2], 0.0),
        )
    )
    joint_max, joint_sum, joint_out = join(parts)
    high, low = split2(joint_out)
    stats = pack_stats(joint_max, joint_sum)
    for near in range(out_ref.shape[0]):
        out_ref[near, 0:QROWS] = high
        out_ref[near, QROWS : 2 * QROWS] = low
        out_ref[near, 2 * QROWS : HROWS] = stats
        for peer in range(peers):
            start = HROWS + peer * piece
            out_ref[near, start : start + piece] = parts_ref[peer, first : first + piece]


def own_kernel(query_ref, key_ref, value_ref, out_ref, stats_ref):
    half = key_ref.shape[0] // 2
    key = key_ref[...]
    values = value_ref[...].T
    causal = lax.broadcasted_iota(jnp.int32, (half, half), 0) <= lax.broadcasted_iota(
        jnp.int32, (half, half), 1
    )
    for j in range(GROUP):
        head = pl.program_id(0) * GROUP + j
        query = query_ref[:, j * HS : (j + 1) * HS]
        early = dot_t(key[:half], query)
        late = dot_t(key[half:], query[half:])
        for part in range(2):
            rows = slice(part * half, (part + 1) * half)
            if part == 0:
                scores = jnp.where(causal, early[:, rows], -jnp.inf)
            else:
                late = jnp.where(causal, late, -jnp.inf)
                scores = jnp.concatenate([early[:, rows], late], axis=0)
            own_max = jnp.max(scores, axis=0, keepdims=True)
            weights = jnp.exp2((scores - own_max) * EXP2_SCALE)
            stats_ref[head, 0:1, rows] = own_max
            stats_ref[head, 1:2, rows] = jnp.sum(weights, axis=0, keepdims=True)
            weighted = dot(values[:, : (part + 1) * half], weights.astype(BF16))
            out_ref[head, :, rows] = weighted.astype(BF16)


def prefill_kernel(query_ref, own_ref, own_stats_ref, anchor_ref, out_ref, decoded_ref):
    group = pl.program_id(0)
    parities = anchor_ref.shape[0] // HK
    piece = (anchor_ref.shape[1] - HROWS) // 2
    use_anchor = lax.axis_index("ctx") != 0
    near = [group * parities + parity for parity in range(parities)]
    keys = jnp.concatenate([anchor_ref[n, HROWS : HROWS + piece] for n in near], axis=0)
    values = jnp.concatenate([anchor_ref[n, HROWS + piece :] for n in near], axis=0).T

    half = out_ref.shape[0] // 2
    units = [(j, slice(part * half, (part + 1) * half)) for j in range(GROUP) for part in range(2)]

    def scores_of(j, rows):
        return dot_t(keys, query_ref[rows, j * HS : (j + 1) * HS])

    def weigh(scores, j, rows):
        head = group * GROUP + j
        own_max, own_sum = own_stats_ref[head, 0:1, rows], own_stats_ref[head, 1:2, rows]
        anchor_max = jnp.max(scores, axis=0, keepdims=True)
        row_max = jnp.where(use_anchor, jnp.maximum(own_max, anchor_max), own_max)
        shift = jnp.where(use_anchor, row_max, jnp.inf)
        weights = jnp.exp2((scores - shift) * EXP2_SCALE)
        own_factor = jnp.exp2((own_max - row_max) * EXP2_SCALE)
        row_sum = own_sum * own_factor + jnp.sum(weights, axis=0, keepdims=True)
        return weights.astype(BF16), own_factor, 1.0 / row_sum

    def finish(weighed, j, rows):
        weights, own_factor, inverse = weighed
        own = own_ref[group * GROUP + j, :, rows].astype(F32)
        weighted = own * own_factor + dot(values, weights)
        out_ref[rows, j * HS : (j + 1) * HS] = (weighted * inverse).T.astype(BF16)

    scores, weighed = scores_of(*units[0]), None
    for at, unit in enumerate(units):
        later = scores_of(*units[at + 1]) if at + 1 < len(units) else None
        weighing = weigh(scores, *unit)
        if weighed is not None:
            finish(weighed, *units[at - 1])
        scores, weighed = later, weighing
    finish(weighed, *units[-1])
    parts = []
    for n in near:
        part_max, part_sum = unpack_stats(anchor_ref[n, 2 * QROWS : HROWS])
        part_out = anchor_ref[n, 0:QROWS].astype(F32) + anchor_ref[n, QROWS : 2 * QROWS].astype(F32)
        parts.append((part_max, part_sum, part_out))
    _, decoded_sum, decoded_out = join(parts)
    decoded = (decoded_out / decoded_sum).astype(BF16)
    for j in range(GROUP):
        pick = (
            lax.broadcasted_iota(jnp.int32, (STEPS, QROWS), 1)
            == lax.broadcasted_iota(jnp.int32, (STEPS, QROWS), 0) + j * STEPS
        )
        decoded_ref[:, j * HS : (j + 1) * HS] = dot(pick.astype(BF16), decoded).astype(BF16)


def rotary_tables(position):
    shape = (PROWS, HS)
    lane = lax.broadcasted_iota(jnp.int32, shape, 1)
    step = lax.broadcasted_iota(jnp.int32, shape, 0) % STEPS
    half_width = HS // 2
    frequency = jnp.exp((lane % half_width).astype(F32) * (-2.0 * math.log(500000.0) / HS))
    angles = (position + step).astype(F32) * frequency
    sine = jnp.sin(angles)
    return jnp.cos(angles), jnp.where(lane < half_width, -sine, sine)


VMEM_SPEC = pl.BlockSpec(memory_space=pltpu.VMEM)


def in_vmem(value):
    return value if INTERPRET else pltpu.with_memory_space_constraint(value, pltpu.VMEM)


def call(kernel, out_shape, **kwargs):
    if not INTERPRET:
        out_shape = jax.tree.map(lambda out: pltpu.VMEM(out.shape, out.dtype), out_shape)
    return pl.pallas_call(
        kernel,
        out_shape=out_shape,
        out_specs=jax.tree.map(lambda _: VMEM_SPEC, out_shape),
        interpret=INTERPRET,
        **kwargs,
    )


def groups_of(contexts):
    far = contexts // NEAR

    def index(x, zz, zo):
        x, zz = (x + HK // 2) % HK, (zz + far // 2) % far
        return (x * far + zz) * PARITIES + zo

    xs, zzs, zos = range(HK), range(far), range(PARITIES)
    near = [[index(x, zz, zo) for x in xs for zo in zos] for zz in zzs]
    return near, [[index(x, zz, zo) for zz in zzs] for x in xs for zo in zos]


def exchange(value, groups):
    return lax.all_to_all(value, "ctx", 0, 0, axis_index_groups=groups, tiled=True)


def layer(ctx_query, ctx_key, ctx_value, step_embed, w_query, w_key, w_value):
    block = ctx_query.shape[0]
    contexts = lax.axis_size("ctx")
    near, far = NEAR, contexts // NEAR
    near_groups, far_groups = groups_of(contexts)
    half = block // PARITIES
    piece = 2 * half // far
    shape = jax.ShapeDtypeStruct
    cosine, sine = rotary_tables(contexts * block)

    slabs = call(
        project_kernel,
        shape((near, 2 * PROWS + 2 * half, HS), BF16),
        name="project",
        scratch_shapes=[pltpu.VMEM((HK, PROWS, HS), F32)],
    )(step_embed, w_query, w_key, w_value, ctx_key, ctx_value)
    cache = in_vmem(exchange(slabs, near_groups))
    spread = call(
        spread_kernel,
        shape((far, 2 * PROWS + piece, HS), BF16),
        name="spread",
        in_specs=[VMEM_SPEC],
    )(cache)
    sums = exchange(spread, far_groups)
    sums = in_vmem(sums)
    width = GROUP * HS
    group_cols = pl.BlockSpec((block, width), lambda h: (0, h))
    head_cols = pl.BlockSpec((block, HS), lambda h: (0, h))
    own, own_stats = call(
        own_kernel,
        (shape((HQ, HS, block), BF16), shape((HQ, 2, block), F32)),
        name="own",
        grid=(HK,),
        in_specs=[group_cols, head_cols, head_cols],
    )(ctx_query, ctx_key, ctx_value)
    parts, new = call(
        decode_kernel,
        (shape((far, QROWS + SROWS + piece, HS), BF16), shape((3, QROWS, HS), F32)),
        name="decode",
        in_specs=[VMEM_SPEC] * 4,
    )(sums, cache, in_vmem(cosine), in_vmem(sine))
    parts = in_vmem(exchange(parts, far_groups))
    heads = call(
        combine_kernel,
        shape((near, HROWS + 2 * half, HS), BF16),
        name="combine",
        in_specs=[VMEM_SPEC] * 2,
    )(parts, in_vmem(new))
    heads = in_vmem(exchange(heads, near_groups))
    context_out, decoded = pl.pallas_call(
        prefill_kernel,
        out_shape=(shape((block, HQ * HS), BF16), shape((STEPS, HQ * HS), BF16)),
        name="prefill",
        grid=(HK,),
        in_specs=[group_cols] + [VMEM_SPEC] * 3,
        out_specs=[
            group_cols,
            pl.BlockSpec((STEPS, width), lambda h: (0, h)),
        ],
        interpret=INTERPRET,
    )(ctx_query, in_vmem(own), in_vmem(own_stats), heads)
    return context_out, decoded


def solution(mesh):
    rows = P(("doc", "ctx"), None)
    return jax.shard_map(
        layer,
        mesh=mesh,
        in_specs=(rows, rows, rows, P("doc", "ctx"), P("ctx", None), P("ctx", None), P("ctx", None)),
        out_specs=(rows, P("doc", None)),
        check_vma=False,
    )
```

```python
import functools
import math

import jax
import jax.numpy as jnp
from jax import lax
from jax.experimental import pallas as pl
from jax.experimental.pallas import tpu as pltpu
from jax.sharding import PartitionSpec as P


HS = 128
HQ = 16
HK = 4
GROUP = 4
STEPS = 4
QROWS = GROUP * STEPS
PROWS = QROWS + 2 * STEPS
SROWS = QROWS // 2
HROWS = 2 * QROWS + SROWS
SCALE = 1.0 / math.sqrt(HS)
EXP2_SCALE = SCALE * math.log2(math.e)
PARITIES = 2
NEAR = HK * PARITIES
BF16 = jnp.bfloat16
F32 = jnp.float32
INTERPRET = False


def dot(a, b):
    return lax.dot_general(a, b, (((1,), (0,)), ((), ())), preferred_element_type=F32)


def dot_t(a, b):
    return lax.dot_general(a, b, (((1,), (1,)), ((), ())), preferred_element_type=F32)


def split2(value):
    high = value.astype(BF16)
    return high, (value - high.astype(F32)).astype(BF16)


def split3(value):
    high = value.astype(BF16)
    rest = value - high.astype(F32)
    middle = rest.astype(BF16)
    return high, middle, (rest - middle.astype(F32)).astype(BF16)


def project_kernel(embed_ref, wq_ref, wk_ref, wv_ref, key_ref, value_ref, out_ref, part_ref):
    parities = out_ref.shape[0] // HK
    half = key_ref.shape[0] // parities
    embed = embed_ref[...]
    query, key, value = dot(embed, wq_ref[...]), dot(embed, wk_ref[...]), dot(embed, wv_ref[...])
    for group in range(HK):
        cols = slice(group * HS, (group + 1) * HS)
        for j in range(GROUP):
            head = group * GROUP + j
            part_ref[group, j * STEPS : (j + 1) * STEPS] = query[:, head * HS : (head + 1) * HS]
        part_ref[group, QROWS : QROWS + STEPS] = key[:, cols]
        part_ref[group, QROWS + STEPS : PROWS] = value[:, cols]
        for parity in range(parities):
            near = group * parities + parity
            rows = slice(parity * half, (parity + 1) * half)
            out_ref[near, 2 * PROWS : 2 * PROWS + half] = key_ref[rows, cols]
            out_ref[near, 2 * PROWS + half : 2 * PROWS + 2 * half] = value_ref[rows, cols]
    for group in range(HK):
        high, low = split2(part_ref[group])
        for parity in range(parities):
            out_ref[group * parities + parity, 0:PROWS] = high
            out_ref[group * parities + parity, PROWS : 2 * PROWS] = low


def add_projections(in_ref):
    total = in_ref[0, 0:PROWS].astype(F32) + in_ref[0, PROWS : 2 * PROWS].astype(F32)
    for source in range(1, in_ref.shape[0]):
        total = total + (
            in_ref[source, 0:PROWS].astype(F32) + in_ref[source, PROWS : 2 * PROWS].astype(F32)
        )
    return total


def spread_kernel(in_ref, out_ref):
    anchor = in_ref.shape[0] // 2
    peers = out_ref.shape[0]
    piece = out_ref.shape[1] - 2 * PROWS
    high, low = split2(add_projections(in_ref))
    for peer in range(peers):
        out_ref[peer, 0:PROWS] = high
        out_ref[peer, PROWS : 2 * PROWS] = low
        start = 2 * PROWS + peer * piece
        out_ref[peer, 2 * PROWS : 2 * PROWS + piece] = in_ref[anchor, start : start + piece]


def pack_stats(part_max, part_sum):
    lane = lax.broadcasted_iota(jnp.int32, (QROWS, HS), 1)
    stats = jnp.zeros((QROWS, HS), F32)
    for at, value in enumerate(split3(part_max) + split3(part_sum)):
        stats = jnp.where(lane == at, value.astype(F32), stats)
    stats = jnp.where(lane[:SROWS] < HS // 2, stats[:SROWS], pltpu.roll(stats[SROWS:], HS // 2, 1))
    return stats.astype(BF16)


def unpack_stats(stats):
    stats = stats.astype(F32)
    stats = jnp.concatenate([stats, pltpu.roll(stats, HS // 2, 1)], axis=0)
    return (
        stats[:, 0:1] + stats[:, 1:2] + stats[:, 2:3],
        stats[:, 3:4] + stats[:, 4:5] + stats[:, 5:6],
    )


def join(parts):
    joint_max = functools.reduce(jnp.maximum, [part[0] for part in parts])
    joint_sum, joint_out = 0.0, 0.0
    for part_max, part_sum, part_out in parts:
        factor = jnp.exp(part_max - joint_max)
        joint_sum = joint_sum + part_sum * factor
        joint_out = joint_out + part_out * factor
    return joint_max, joint_sum, joint_out


def decode_kernel(sums_ref, cache_ref, cos_ref, sin_ref, out_ref, new_ref):
    peers = sums_ref.shape[0]
    half = (cache_ref.shape[1] - 2 * PROWS) // 2
    piece = sums_ref.shape[1] - 2 * PROWS
    total = add_projections(sums_ref)
    rotated = total * cos_ref[...] + pltpu.roll(total, HS // 2, 1) * sin_ref[...]
    query = rotated[0:QROWS].astype(BF16)
    sources = range(cache_ref.shape[0])
    scores = jnp.concatenate(
        [dot_t(query, cache_ref[c, 2 * PROWS : 2 * PROWS + half]) for c in sources], axis=1
    )
    scores = scores * SCALE
    joint_max = jnp.max(scores, axis=1, keepdims=True)
    weights = jnp.exp(scores - joint_max)
    joint_sum = jnp.sum(weights, axis=1, keepdims=True)
    weights = weights.astype(BF16)
    joint_out = functools.reduce(
        jnp.add,
        [
            dot(weights[:, c * half : (c + 1) * half], cache_ref[c, 2 * PROWS + half :])
            for c in sources
        ],
    )
    stats = pack_stats(joint_max, joint_sum)
    joint_out = joint_out.astype(BF16)
    anchor = sums_ref[1, 2 * PROWS : 2 * PROWS + piece]
    for peer in range(peers):
        out_ref[peer, 0:QROWS] = joint_out
        out_ref[peer, QROWS : QROWS + SROWS] = stats
        out_ref[peer, QROWS + SROWS : QROWS + SROWS + piece] = anchor
    key_new = rotated[QROWS:PROWS].astype(BF16)
    value_new = pltpu.roll(total[QROWS:PROWS], STEPS, 0).astype(BF16)
    scores = dot_t(query, key_new) * SCALE
    step = lax.broadcasted_iota(jnp.int32, scores.shape, 0) % STEPS
    later = lax.broadcasted_iota(jnp.int32, scores.shape, 1)
    scores = jnp.where(later <= step, scores, -jnp.inf)
    new_max = jnp.max(scores, axis=1, keepdims=True)
    weights = jnp.exp(scores - new_max)
    new_sum = jnp.sum(weights, axis=1, keepdims=True)
    new_ref[0] = jnp.broadcast_to(new_max, (QROWS, HS))
    new_ref[1] = jnp.broadcast_to(new_sum, (QROWS, HS))
    new_ref[2] = dot(weights.astype(BF16), value_new)


def combine_kernel(parts_ref, new_ref, out_ref):
    peers = parts_ref.shape[0]
    first = QROWS + SROWS
    piece = parts_ref.shape[1] - first
    parts = []
    for peer in range(peers):
        part_max, part_sum = unpack_stats(parts_ref[peer, QROWS:first])
        parts.append((part_max, part_sum, parts_ref[peer, 0:QROWS].astype(F32)))
    has_new = lax.axis_index("ctx") % PARITIES == 0
    new_max = new_ref[0][:, 0:1]
    parts.append(
        (
            jnp.where(has_new, new_max, parts[0][0]),
            jnp.where(has_new, new_ref[1][:, 0:1], 0.0),
            jnp.where(has_new, new_ref[2], 0.0),
        )
    )
    joint_max, joint_sum, joint_out = join(parts)
    high, low = split2(joint_out)
    stats = pack_stats(joint_max, joint_sum)
    for near in range(out_ref.shape[0]):
        out_ref[near, 0:QROWS] = high
        out_ref[near, QROWS : 2 * QROWS] = low
        out_ref[near, 2 * QROWS : HROWS] = stats
        for peer in range(peers):
            start = HROWS + peer * piece
            out_ref[near, start : start + piece] = parts_ref[peer, first : first + piece]


def own_kernel(query_ref, key_ref, value_ref, out_ref, stats_ref):
    half = key_ref.shape[0] // 2
    key = key_ref[...]
    values = value_ref[...].T
    causal = lax.broadcasted_iota(jnp.int32, (half, half), 0) <= lax.broadcasted_iota(
        jnp.int32, (half, half), 1
    )
    for j in range(GROUP):
        head = pl.program_id(0) * GROUP + j
        query = query_ref[:, j * HS : (j + 1) * HS]
        early = dot_t(key[:half], query)
        late = dot_t(key[half:], query[half:])
        for part in range(2):
            rows = slice(part * half, (part + 1) * half)
            if part == 0:
                scores = jnp.where(causal, early[:, rows], -jnp.inf)
            else:
                late = jnp.where(causal, late, -jnp.inf)
                scores = jnp.concatenate([early[:, rows], late], axis=0)
            own_max = jnp.max(scores, axis=0, keepdims=True)
            weights = jnp.exp2((scores - own_max) * EXP2_SCALE)
            stats_ref[head, 0:1, rows] = own_max
            stats_ref[head, 1:2, rows] = jnp.sum(weights, axis=0, keepdims=True)
            weighted = dot(values[:, : (part + 1) * half], weights.astype(BF16))
            out_ref[head, :, rows] = weighted.astype(BF16)


def prefill_kernel(query_ref, own_ref, own_stats_ref, anchor_ref, out_ref, decoded_ref):
    group = pl.program_id(0)
    parities = anchor_ref.shape[0] // HK
    piece = (anchor_ref.shape[1] - HROWS) // 2
    use_anchor = lax.axis_index("ctx") != 0
    near = [group * parities + parity for parity in range(parities)]
    keys = jnp.concatenate([anchor_ref[n, HROWS : HROWS + piece] for n in near], axis=0)
    values = jnp.concatenate([anchor_ref[n, HROWS + piece :] for n in near], axis=0).T

    half = out_ref.shape[0] // 2
    units = [(j, slice(part * half, (part + 1) * half)) for j in range(GROUP) for part in range(2)]

    def scores_of(j, rows):
        return dot_t(keys, query_ref[rows, j * HS : (j + 1) * HS])

    def weigh(scores, j, rows):
        head = group * GROUP + j
        own_max, own_sum = own_stats_ref[head, 0:1, rows], own_stats_ref[head, 1:2, rows]
        anchor_max = jnp.max(scores, axis=0, keepdims=True)
        row_max = jnp.where(use_anchor, jnp.maximum(own_max, anchor_max), own_max)
        shift = jnp.where(use_anchor, row_max, jnp.inf)
        weights = jnp.exp2((scores - shift) * EXP2_SCALE)
        own_factor = jnp.exp2((own_max - row_max) * EXP2_SCALE)
        row_sum = own_sum * own_factor + jnp.sum(weights, axis=0, keepdims=True)
        return weights.astype(BF16), own_factor, 1.0 / row_sum

    def finish(weighed, j, rows):
        weights, own_factor, inverse = weighed
        own = own_ref[group * GROUP + j, :, rows].astype(F32)
        weighted = own * own_factor + dot(values, weights)
        out_ref[rows, j * HS : (j + 1) * HS] = (weighted * inverse).T.astype(BF16)

    scores, weighed = scores_of(*units[0]), None
    for at, unit in enumerate(units):
        later = scores_of(*units[at + 1]) if at + 1 < len(units) else None
        weighing = weigh(scores, *unit)
        if weighed is not None:
            finish(weighed, *units[at - 1])
        scores, weighed = later, weighing
    finish(weighed, *units[-1])
    parts = []
    for n in near:
        part_max, part_sum = unpack_stats(anchor_ref[n, 2 * QROWS : HROWS])
        part_out = anchor_ref[n, 0:QROWS].astype(F32) + anchor_ref[n, QROWS : 2 * QROWS].astype(F32)
        parts.append((part_max, part_sum, part_out))
    _, decoded_sum, decoded_out = join(parts)
    decoded = (decoded_out / decoded_sum).astype(BF16)
    for j in range(GROUP):
        pick = (
            lax.broadcasted_iota(jnp.int32, (STEPS, QROWS), 1)
            == lax.broadcasted_iota(jnp.int32, (STEPS, QROWS), 0) + j * STEPS
        )
        decoded_ref[:, j * HS : (j + 1) * HS] = dot(pick.astype(BF16), decoded).astype(BF16)


def rotary_tables(position):
    shape = (PROWS, HS)
    lane = lax.broadcasted_iota(jnp.int32, shape, 1)
    step = lax.broadcasted_iota(jnp.int32, shape, 0) % STEPS
    half_width = HS // 2
    frequency = jnp.exp((lane % half_width).astype(F32) * (-2.0 * math.log(500000.0) / HS))
    angles = (position + step).astype(F32) * frequency
    sine = jnp.sin(angles)
    return jnp.cos(angles), jnp.where(lane < half_width, -sine, sine)


VMEM_SPEC = pl.BlockSpec(memory_space=pltpu.VMEM)


def in_vmem(value):
    return value if INTERPRET else pltpu.with_memory_space_constraint(value, pltpu.VMEM)


def call(kernel, out_shape, **kwargs):
    if not INTERPRET:
        out_shape = jax.tree.map(lambda out: pltpu.VMEM(out.shape, out.dtype), out_shape)
    return pl.pallas_call(
        kernel,
        out_shape=out_shape,
        out_specs=jax.tree.map(lambda _: VMEM_SPEC, out_shape),
        interpret=INTERPRET,
        **kwargs,
    )


def groups_of(contexts):
    far = contexts // NEAR
    middle = far // 2

    def index(x, zz, zo):
        return (x * far + zz) * PARITIES + zo

    xs, zos = [(x + HK // 2) % HK for x in range(HK)], range(PARITIES)
    rest = [zz for zz in range(far) if zz != middle]
    zzs = [middle] + sorted(rest, key=lambda zz: min(zz, far - zz))
    near = [[index(x, zz, zo) for x in xs for zo in zos] for zz in zzs]
    return near, [[index(x, zz, zo) for zz in zzs] for x in xs for zo in zos]


def exchange(value, groups):
    return lax.all_to_all(value, "ctx", 0, 0, axis_index_groups=groups, tiled=True)


def layer(ctx_query, ctx_key, ctx_value, step_embed, w_query, w_key, w_value):
    block = ctx_query.shape[0]
    contexts = lax.axis_size("ctx")
    near, far = NEAR, contexts // NEAR
    near_groups, far_groups = groups_of(contexts)
    half = block // PARITIES
    piece = 2 * half // far
    shape = jax.ShapeDtypeStruct
    cosine, sine = rotary_tables(contexts * block)

    slabs = call(
        project_kernel,
        shape((near, 2 * PROWS + 2 * half, HS), BF16),
        name="project",
        scratch_shapes=[pltpu.VMEM((HK, PROWS, HS), F32)],
    )(step_embed, w_query, w_key, w_value, ctx_key, ctx_value)
    cache = in_vmem(exchange(slabs, near_groups))
    spread = call(
        spread_kernel,
        shape((far, 2 * PROWS + piece, HS), BF16),
        name="spread",
        in_specs=[VMEM_SPEC],
    )(cache)
    sums = exchange(spread, far_groups)
    sums = in_vmem(sums)
    width = GROUP * HS
    group_cols = pl.BlockSpec((block, width), lambda h: (0, h))
    head_cols = pl.BlockSpec((block, HS), lambda h: (0, h))
    own, own_stats = call(
        own_kernel,
        (shape((HQ, HS, block), BF16), shape((HQ, 2, block), F32)),
        name="own",
        compiler_params=pltpu.CompilerParams(),
        grid=(HK,),
        in_specs=[group_cols, head_cols, head_cols],
    )(ctx_query, ctx_key, ctx_value)
    parts, new = call(
        decode_kernel,
        (shape((far, QROWS + SROWS + piece, HS), BF16), shape((3, QROWS, HS), F32)),
        name="decode",
        in_specs=[VMEM_SPEC] * 4,
    )(sums, cache, in_vmem(cosine), in_vmem(sine))
    parts = in_vmem(exchange(parts, far_groups))
    heads = call(
        combine_kernel,
        shape((near, HROWS + 2 * half, HS), BF16),
        name="combine",
        in_specs=[VMEM_SPEC] * 2,
    )(parts, in_vmem(new))
    heads = in_vmem(exchange(heads, near_groups))
    context_out, decoded = pl.pallas_call(
        prefill_kernel,
        out_shape=(shape((block, HQ * HS), BF16), shape((STEPS, HQ * HS), BF16)),
        name="prefill",
        grid=(HK,),
        in_specs=[group_cols] + [VMEM_SPEC] * 3,
        out_specs=[
            group_cols,
            pl.BlockSpec((STEPS, width), lambda h: (0, h)),
        ],
        interpret=INTERPRET,
    )(ctx_query, in_vmem(own), in_vmem(own_stats), heads)
    return context_out, decoded


def solution(mesh):
    rows = P(("doc", "ctx"), None)
    return jax.shard_map(
        layer,
        mesh=mesh,
        in_specs=(rows, rows, rows, P("doc", "ctx"), P("ctx", None), P("ctx", None), P("ctx", None)),
        out_specs=(rows, P("doc", None)),
        check_vma=False,
    )
```
